32 devices in a mesh: row: 4 (over z), col: 8 (over y, x, core).
Axes of the slice: x: 2, y: 2, z: 4, core: 2. Of those that a mesh axis runs over, the one named last changes fastest.
Arguments:
- cotangent: float32 [4096, 8192], P('row', 'col'), may hold values from -6 to 6
- whitened: float32 [4096, 8192], P('row', 'col'), may hold values from -0.0625 to 0.0625
- panel_rows: float32 [4, 256, 4096], P(None, None, 'row'), may hold values from -0.375 to 0.375
- diag_inverse: float32 [4, 256, 256], replicated, as said below
Outputs:
- adjoint_rhs: float32 [4096, 8192], P('row', 'col')
- factor_grad: float32 [4, 256, 4096], P(None, 'col', 'row')
The draws below stay inside these ranges and needn't reach their ends.
Inputs may be any that keep to these rules, and one draw needn't show every extreme that they name: `diag_inverse`: each block is lower triangular with diagonal entries between 0.5 and 1.5.
All inputs are finite; a program needn't handle non-finite values.
Results may differ from the reference program's by a relative error of at most 0.00017.
Values sent between devices are 32-bit elements; how exact they have to be, the bound alone decides.
A program may use at most 128 MiB of HBM per device.

```python
import math
import jax
import jax.numpy as jnp
from jax import lax

NB = 256
PANELS = 4
ROWS_DEV = 1024
M = 4096
RHS = 8192
N_ROW = 4


def draw_diag_inverse(key, part):
    first, second = jax.random.split(jax.random.fold_in(key, 17))
    lower = jax.random.normal(first, (PANELS, NB, NB), jnp.float32) / math.sqrt(NB)
    diagonal = jax.random.uniform(second, (PANELS, NB), jnp.float32, 0.5, 1.5)
    return jnp.tril(lower, -1) + diagonal[:, :, None] * jnp.eye(NB, dtype=jnp.float32)[None]


def steps_of(key, extent, cuts, smallest, largest):
    def one(dim, blocks):
        draws = jax.random.uniform(jax.random.fold_in(jax.random.fold_in(key, 6), dim), (blocks,), jnp.float32, smallest / len(cuts), largest / len(cuts))
        return jnp.repeat(jnp.exp(draws), extent[dim] // blocks).reshape((-1,) + (1,) * (len(extent) - dim - 1))

    level = one(*cuts[0])
    for cut in cuts[1:]:
        level = level * one(*cut)
    return level


def centred(own_key, extent, scale, reach, pieces=(), kind=jnp.bfloat16):
    gain = steps_of(own_key, extent, pieces, -0.22, 0.18) if pieces else 1.0
    result = jax.random.normal(own_key, extent, jnp.float32) * scale * gain
    return jnp.minimum(jnp.maximum(result, -reach), reach).astype(kind)


def setup_inputs(seed: int = 0) -> dict:
    key_of = jax.random.split(jax.random.key(seed), 5)
    cotangent = centred(key_of[0], (M, RHS), 1.0, 6.0, ((0, 4), (1, 8)), jnp.float32)
    whitened = centred(key_of[1], (M, RHS), RHS ** -0.5, 0.0625, ((0, 4), (1, 8)), jnp.float32)
    panel_rows = centred(key_of[2], (PANELS, NB, M), NB ** -0.5, 0.375, ((2, 4),), jnp.float32)
    diag_inverse = draw_diag_inverse(jax.random.fold_in(key_of[4], 71), 0)
    return {"cotangent": cotangent, "whitened": whitened, "panel_rows": panel_rows, "diag_inverse": diag_inverse}


def reference(cotangent, whitened, panel_rows, diag_inverse):
    hi = lax.Precision.HIGHEST
    stored = jnp.arange(M, dtype=jnp.int32)
    natural = ((stored % ROWS_DEV) // NB) * N_ROW + stored // ROWS_DEV
    within = stored % NB
    inner = jnp.arange(NB, dtype=jnp.int32)
    blocks = M // NB
    residual = cotangent
    grads = []
    for p in range(PANELS):
        target = blocks - 1 - p
        start = (N_ROW - 1 - p) * ROWS_DEV + ROWS_DEV - NB
        solved = jnp.dot(diag_inverse[p].T, residual[start:start + NB], precision=hi, preferred_element_type=jnp.float32)
        masked = jnp.where((natural < target)[None, :], panel_rows[p], 0.0)
        update = lax.dot_general(masked, solved, (((0,), (0,)), ((), ())), precision=hi, preferred_element_type=jnp.float32)
        residual = residual - update
        residual = jnp.concatenate([residual[:start], solved, residual[start + NB:]], 0)
        term = lax.dot_general(solved, whitened, (((1,), (1,)), ((), ())), precision=hi, preferred_element_type=jnp.float32)
        keep = (natural[None, :] < target) | ((natural[None, :] == target) & (inner[:, None] >= within[None, :]))
        grads.append(-jnp.where(keep, term, 0.0))
    return residual, jnp.stack(grads)
```

```python
import functools

import jax
import jax.numpy as jnp
from jax import lax
from jax.experimental import pallas as pl
from jax.experimental.pallas import tpu as pltpu
from jax.sharding import PartitionSpec as P

MESH = pl.DeviceIdType.MESH
CHUNK = 128
PIECES = 2
LAG = 3
F32 = jnp.float32
BF16 = jnp.bfloat16


def split(x):
    hi = x.astype(BF16)
    return hi, (x - hi.astype(F32)).astype(BF16)


def product(a, b, dims):
    dot = functools.partial(lax.dot_general, dimension_numbers=(dims, ((), ())), preferred_element_type=F32)
    return dot(a[0], b[0]) + (dot(a[0], b[1]) + dot(a[1], b[0]))


NN = ((1,), (0,))
NT = ((1,), (1,))


def kernel(
    n_row, n_col, cot_hbm, wht_hbm, pan_hbm, diag_hbm, res_ref, out_ref,
    wht_ref, pan_ref, diag_ref, y, pth, ptl, dth, dtl, wh, wl, grad, rs_a, rs_b,
    far_pan, far_own, fph, fpl,
    local_sem, recv_sem, down_sem, up_sem, a_send, a_recv, b_send, b_recv, fp_send, fp_recv, fo_send, fo_recv,
):
    rows, rhs = res_ref.shape
    panels, width = diag_ref.shape[0], diag_ref.shape[1]
    count = rhs // CHUNK
    blocks = rows // width
    tail = rows - width
    part = width // n_col
    chips = n_col // 2
    piece = width // PIECES
    row, col = lax.axis_index("row"), lax.axis_index("col")
    core, chip = lax.rem(col, 2), col // 2
    last = panels - 1
    last_root = n_row - panels
    helper = last_root + 1

    def columns(c):
        return pl.ds(pl.multiple_of(c * CHUNK, CHUNK), CHUNK)

    def y_copy(p, c, h, sems, step):
        block = y.at[p, c, h * piece : (h + 1) * piece]
        return pltpu.make_async_remote_copy(
            src_ref=block, dst_ref=block, send_sem=sems.at[p], recv_sem=recv_sem.at[p, c, h],
            device_id={"row": lax.rem(row + step, n_row)}, device_id_type=MESH,
        )

    def down(p, c, h):
        return y_copy(p, c, h, down_sem, n_row - 1)

    def up(p, c, h):
        return y_copy(p, c, h, up_sem, 1)

    def far_panel(p):
        return pltpu.make_async_remote_copy(
            src_ref=pan_hbm.at[p, :, tail:], dst_ref=far_pan.at[p], send_sem=fp_send, recv_sem=fp_recv,
            device_id={"row": lax.rem(row + 1, n_row)}, device_id_type=MESH,
        )

    def far_rows(c):
        return pltpu.make_async_remote_copy(
            src_ref=cot_hbm.at[tail:, columns(c)], dst_ref=far_own.at[c], send_sem=fo_send, recv_sem=fo_recv.at[c],
            device_id={"row": lax.rem(row + 1, n_row)}, device_id_type=MESH,
        )

    def group(g):
        return slice(0, blocks - 1) if g == 0 else slice(blocks - 1, blocks)

    def pair_copy(p, m, g):
        place = (2 * m + 1 - core) * part
        return pltpu.make_async_remote_copy(
            src_ref=grad.at[p, group(g), pl.ds(pl.multiple_of(place, part), part)], dst_ref=rs_a.at[p, m, group(g)],
            send_sem=a_send.at[p, g], recv_sem=a_recv.at[p, g],
            device_id={"col": 2 * chip + 1 - core}, device_id_type=MESH,
        )

    def chip_copy(p, j, g):
        peer = lax.rem(chip + j, chips)
        return pltpu.make_async_remote_copy(
            src_ref=rs_a.at[p, peer, group(g)], dst_ref=rs_b.at[p, j, group(g)],
            send_sem=b_send.at[p, g], recv_sem=b_recv.at[p, g],
            device_id={"col": 2 * peer + core}, device_id_type=MESH,
        )

    def pair_all(p, g):
        return pltpu.make_async_remote_copy(
            src_ref=rs_a.at[p, :, group(g)], dst_ref=rs_a.at[p, :, group(g)],
            send_sem=a_send.at[p, g], recv_sem=a_recv.at[p, g],
            device_id={"col": 2 * chip + 1 - core}, device_id_type=MESH,
        )

    def chip_all(p, g):
        return pltpu.make_async_remote_copy(
            src_ref=rs_b.at[p, 1:, group(g)], dst_ref=rs_b.at[p, 1:, group(g)],
            send_sem=b_send.at[p, g], recv_sem=b_recv.at[p, g],
            device_id={"col": 2 * lax.rem(chip + 1, chips) + core}, device_id_type=MESH,
        )

    def y_all(p, sems, step):
        return pltpu.make_async_remote_copy(
            src_ref=y.at[p], dst_ref=y.at[p], send_sem=sems.at[p], recv_sem=recv_sem.at[p, 0, 0],
            device_id={"row": lax.rem(row + step, n_row)}, device_id_type=MESH,
        )

    def far_all():
        return pltpu.make_async_remote_copy(
            src_ref=far_pan, dst_ref=far_pan, send_sem=fp_send, recv_sem=fp_recv,
            device_id={"row": lax.rem(row + 1, n_row)}, device_id_type=MESH,
        )

    def own_all():
        return pltpu.make_async_remote_copy(
            src_ref=far_own, dst_ref=far_own, send_sem=fo_send, recv_sem=fo_recv.at[0],
            device_id={"row": lax.rem(row + 1, n_row)}, device_id_type=MESH,
        )

    def groups(p, act):
        act(0)

        @pl.when(row <= n_row - 1 - p)
        def _():
            act(1)

    def pair_start(p):
        @pl.when(row == n_row - 1 - p)
        def _():
            inner = lax.broadcasted_iota(jnp.int32, (width, width), 0)
            within = lax.broadcasted_iota(jnp.int32, (width, width), 1)
            grad[p, blocks - 1] = jnp.where(inner >= within, grad[p, blocks - 1], 0.0)

        def act(g):
            for m in range(chips):
                pair_copy(p, m, g).start()

        groups(p, act)

    def chip_start(p):
        def act(g):
            pair_all(p, g).wait_recv()
            for m in range(chips):
                place = pl.multiple_of((2 * m + core) * part, part)
                rs_a[p, m, group(g)] += grad[p, group(g), pl.ds(place, part)]
            for j in range(1, chips):
                chip_copy(p, j, g).start()

        groups(p, act)

    def finish(p):
        def act(g):
            chip_all(p, g).wait_recv()
            for b in range(blocks)[group(g)]:
                total = rs_a[p, chip, b]
                for j in range(1, chips):
                    total = total + rs_b[p, j, b]
                out_ref[p, :, b * width : (b + 1) * width] = total

        out_ref[p, :, tail:] = jnp.zeros((part, width), F32)
        groups(p, act)

    def solve(p, c, own):
        y[p, c] = product((dth[p], dtl[p]), split(own), NN)

    def inverse(p):
        hi, lo = split(diag_ref[p].T)
        dth[p] = hi
        dtl[p] = lo

    def receive(p, c):
        root = n_row - 1 - p
        source = row == root
        if p == last:
            source = source | (row == helper)
        for h in range(PIECES):
            @pl.when(jnp.logical_not(source))
            def _():
                y_copy(p, c, h, down_sem, n_row - 1).wait_recv()

            @pl.when(jnp.logical_not(source) & (row > root) & (row < n_row - 1))
            def _():
                up(p, c, h).start()

            @pl.when((row > 0) & (row < root))
            def _():
                down(p, c, h).start()

    def send(p, c, way):
        for h in range(PIECES):
            way(p, c, h).start()

    def tail_update(p, c):
        res_ref[tail:, columns(c)] -= product((pth[p, tail:], ptl[p, tail:]), split(y[p, c]), NN)

    def keep(p, c):
        @pl.when(row == n_row - 1 - p)
        def _():
            res_ref[tail:, columns(c)] = y[p, c]

    def grad_work(q, c):
        yq = split(y[q, c])
        for b in range(blocks):
            at = slice(b * width, (b + 1) * width)
            grad[q, b] -= product(yq, (wh[c, at], wl[c, at]), NT)

    def res_work(q, c):
        yq = split(y[q, c])
        for b in range(blocks - 1):
            at = slice(b * width, (b + 1) * width)
            res_ref[at, columns(c)] -= product((pth[q, at], ptl[q, at]), yq, NN)

    def far(c):
        far_rows(c).wait_recv()
        own = far_own[c]
        for p in range(last):
            own = own - product((fph[p], fpl[p]), split(y[p, c]), NN)
        solve(last, c, own)
        send(last, c, up)

    barrier = pltpu.get_barrier_semaphore()
    for step in (1, n_row - 1):
        pl.semaphore_signal(barrier, inc=1, device_id={"row": lax.rem(row + step, n_row)}, device_id_type=MESH)
    for step in range(1, n_col):
        pl.semaphore_signal(barrier, inc=1, device_id={"col": lax.rem(col + step, n_col)}, device_id_type=MESH)

    diag_copy = pltpu.make_async_copy(diag_hbm, diag_ref, local_sem.at[0])
    tail_copy = pltpu.make_async_copy(cot_hbm.at[tail:], res_ref.at[tail:], local_sem.at[1])
    pan_copy = pltpu.make_async_copy(pan_hbm, pan_ref, local_sem.at[2])
    head_copy = pltpu.make_async_copy(cot_hbm.at[:tail], res_ref.at[:tail], local_sem.at[3])
    wht_copy = pltpu.make_async_copy(wht_hbm, wht_ref, local_sem.at[4])
    for copy in (diag_copy, tail_copy, pan_copy, wht_copy, head_copy):
        copy.start()
    diag_copy.wait()
    inverse(0)
    tail_copy.wait()
    pl.semaphore_wait(barrier, 2 + n_col - 1)

    @pl.when(row == n_row - 1)
    def _():
        @pl.loop(0, count)
        def _(c):
            solve(0, c, res_ref[tail:, columns(c)])
            send(0, c, down)

    @pl.when(row == last_root)
    def _():
        @pl.loop(0, last)
        def _(p):
            far_panel(p).start()

        @pl.loop(0, count)
        def _(c):
            far_rows(c).start()

    @pl.loop(1, panels)
    def _(p):
        inverse(p)

    pan_copy.wait()

    @pl.loop(0, panels)
    def _(p):
        for b in range(blocks):
            hi, lo = split(pan_ref[p, :, b * width : (b + 1) * width].T)
            pth[p, b * width : (b + 1) * width] = hi
            ptl[p, b * width : (b + 1) * width] = lo
        grad[p] = jnp.zeros(grad.shape[1:], F32)

    wht_copy.wait()
    head_copy.wait()

    @pl.loop(0, count)
    def _(c):
        for p in range(last - 1):
            root = n_row - 1 - p
            receive(p, c)

            @pl.when(row < root)
            def _():
                tail_update(p, c)

                @pl.when(row == root - 1)
                def _():
                    solve(p + 1, c, res_ref[tail:, columns(c)])
                    send(p + 1, c, up)
                    if p + 1 < last - 1:
                        send(p + 1, c, down)

            keep(p, c)

        hi, lo = split(wht_ref[:, columns(c)])
        wh[c] = hi
        wl[c] = lo

        end = jnp.where(row == helper, last, last - 1)

        @pl.loop(0, end)
        def _(q):
            grad_work(q, c)
            res_work(q, c)

        @pl.when((row == helper) & (c == LAG))
        def _():
            far_all().wait_recv()

            @pl.loop(0, last)
            def _(p):
                hi, lo = split(far_pan[p].T)
                fph[p] = hi
                fpl[p] = lo

        @pl.when((row == helper) & (c >= LAG))
        def _():
            far(c - LAG)

    @pl.when(row == helper)
    def _():
        @pl.loop(0, count)
        def _(c):
            send(last - 1, c, down)

        @pl.loop(count - LAG, count)
        def _(c):
            far(c)

    for p in range(last - 1):
        pair_start(p)

    @pl.when(row == helper)
    def _():
        pair_start(last - 1)

    lag = jnp.where(row > helper, LAG, 0)

    @pl.loop(0, count + lag)
    def _(t):
        @pl.when((row != helper) & (t < count))
        def _():
            receive(last - 1, t)

            @pl.when(row < helper)
            def _():
                tail_update(last - 1, t)

                @pl.when(row == last_root)
                def _():
                    solve(last, t, res_ref[tail:, columns(t)])

                    @pl.when(row > 0)
                    def _():
                        send(last, t, down)

        @pl.when(t < count)
        def _():
            keep(last - 1, t)

        c = t - lag

        @pl.when(c >= 0)
        def _():
            receive(last, c)

            @pl.when(row < last_root)
            def _():
                tail_update(last, c)

            keep(last, c)

        @pl.when((row != helper) & (t < count))
        def _():
            grad_work(last - 1, t)

            @pl.when(t == count - 1)
            def _():
                pair_start(last - 1)

        @pl.when(c >= 0)
        def _():
            grad_work(last, c)

            @pl.when(c == count - 1)
            def _():
                pair_start(last)

        @pl.when((row != helper) & (t < count))
        def _():
            res_work(last - 1, t)

        @pl.when(c >= 0)
        def _():
            res_work(last, c)

        for p in range(last - 1):
            @pl.when(t == 1 + p)
            def _():
                chip_start(p)

            @pl.when(t == count - 3 + p)
            def _():
                finish(p)

        @pl.when((t == count + 1) | ((row == helper) & (t == count // 2)))
        def _():
            chip_start(last - 1)

    @pl.when(row < helper)
    def _():
        chip_start(last - 1)

    chip_start(last)
    finish(last - 1)
    finish(last)

    @pl.loop(0, panels)
    def _(p):
        root = n_row - 1 - p

        def act(g):
            pair_all(p, g).wait_send()
            chip_all(p, g).wait_send()

        groups(p, act)

        @pl.when((row >= root) & (row < n_row - 1) & ((p < last) | (row > last_root)))
        def _():
            y_all(p, up_sem, 1).wait_send()

        @pl.when((row <= root) & (row > 0))
        def _():
            y_all(p, down_sem, n_row - 1).wait_send()

    @pl.when(row == last_root)
    def _():
        far_all().wait_send()
        own_all().wait_send()


def store_kernel(res_ref, grad_ref, res_hbm, grad_hbm, sems):
    copies = (
        pltpu.make_async_copy(res_ref, res_hbm, sems.at[0]),
        pltpu.make_async_copy(grad_ref, grad_hbm, sems.at[1]),
    )
    for copy in copies:
        copy.start()
    for copy in copies:
        copy.wait()


def solution(mesh):
    n_row, n_col = mesh.shape["row"], mesh.shape["col"]

    def body(cotangent, whitened, panel_rows, diag_inverse):
        rows, rhs = cotangent.shape
        panels, width = diag_inverse.shape[:2]
        assert 3 <= panels <= n_row and n_col % 2 == 0 and rhs // CHUNK > LAG + 2
        count, blocks, part, chips = rhs // CHUNK, rows // width, width // n_col, n_col // 2
        anywhere = pl.BlockSpec(memory_space=pl.ANY)
        vmem = pl.BlockSpec(memory_space=pltpu.VMEM)
        hbm = pl.BlockSpec(memory_space=pltpu.HBM)
        dma = pltpu.SemaphoreType.DMA
        kept = pl.pallas_call(
            functools.partial(kernel, n_row, n_col),
            out_shape=(pltpu.VMEM((rows, rhs), F32), pltpu.VMEM((panels, part, rows), F32)),
            in_specs=[hbm] * 4,
            out_specs=(vmem, vmem),
            scratch_shapes=[
                pltpu.VMEM((rows, rhs), F32),
                pltpu.VMEM((panels, width, rows), F32),
                pltpu.VMEM((panels, width, width), F32),
                pltpu.VMEM((panels, count, width, CHUNK), F32),
                pltpu.VMEM((panels, rows, width), BF16),
                pltpu.VMEM((panels, rows, width), BF16),
                pltpu.VMEM((panels, width, width), BF16),
                pltpu.VMEM((panels, width, width), BF16),
                pltpu.VMEM((count, rows, CHUNK), BF16),
                pltpu.VMEM((count, rows, CHUNK), BF16),
                pltpu.VMEM((panels, blocks, width, width), F32),
                pltpu.VMEM((panels, chips, blocks, part, width), F32),
                pltpu.VMEM((panels, chips, blocks, part, width), F32),
                pltpu.VMEM((panels - 1, width, width), F32),
                pltpu.VMEM((count, width, CHUNK), F32),
                pltpu.VMEM((panels - 1, width, width), BF16),
                pltpu.VMEM((panels - 1, width, width), BF16),
                dma((5,)),
                dma((panels, count, PIECES)),
                dma((panels,)),
                dma((panels,)),
                dma((panels, 2)),
                dma((panels, 2)),
                dma((panels, 2)),
                dma((panels, 2)),
                dma,
                dma,
                dma,
                dma((count,)),
            ],
            compiler_params=pltpu.CompilerParams(
                collective_id=0, has_side_effects=True, vmem_limit_bytes=117 * 512 * 1024
            ),
        )(cotangent, whitened, panel_rows, diag_inverse)
        return pl.pallas_call(
            store_kernel,
            out_shape=tuple(jax.ShapeDtypeStruct(k.shape, F32) for k in kept),
            in_specs=[anywhere] * 2,
            out_specs=(hbm, hbm),
            scratch_shapes=[dma((2,))],
            compiler_params=pltpu.CompilerParams(vmem_limit_bytes=1024 * 1024),
        )(*kept)

    return jax.shard_map(
        body,
        mesh=mesh,
        in_specs=(P("row", "col"), P("row", "col"), P(None, None, "row"), P()),
        out_specs=(P("row", "col"), P(None, "col", "row")),
        check_vma=False,
    )
```

```python
import functools

import jax
import jax.numpy as jnp
from jax import lax
from jax.experimental import pallas as pl
from jax.experimental.pallas import tpu as pltpu
from jax.sharding import PartitionSpec as P

MESH = pl.DeviceIdType.MESH
CHUNK = 256
PIECES = 4
STORES = 4
RAW = (0, 2)
LATE = 1
F32 = jnp.float32
BF16 = jnp.bfloat16


def split(x):
    hi = x.astype(BF16)
    return hi, (x - hi.astype(F32)).astype(BF16)


def product(a, b, dims):
    dot = functools.partial(lax.dot_general, dimension_numbers=(dims, ((), ())), preferred_element_type=F32)
    return dot(a[0], b[0]) + (dot(a[0], b[1]) + dot(a[1], b[0]))


NN = ((1,), (0,))
NT = ((1,), (1,))


def kernel(
    n_row, n_col, cot_hbm, wht_hbm, pan_hbm, diag_hbm, res_ref, out_ref,
    wht_ref, pan_ref, diag_ref, y, pth, ptl, dth, dtl, wh, wl, grad, rs_a, rs_b,
    far_pan, far_own, fph, fpl, late_w, late_out, late_in,
    local_sem, recv_sem, down_sem, up_sem, a_send, a_recv, b_send, b_recv,
    fp_send, fp_recv, fo_send, fo_recv, ag_send, ag_recv, lw_send, lw_recv, lr_send, lr_recv,
):
    rows, rhs = res_ref.shape
    panels, width = diag_ref.shape[0], diag_ref.shape[1]
    count = rhs // CHUNK
    blocks = rows // width
    tail = rows - width
    part = width // n_col
    chips = n_col // 2
    piece = width // PIECES
    row, col = lax.axis_index("row"), lax.axis_index("col")
    core, chip = lax.rem(col, 2), col // 2
    last = panels - 1
    last_root = n_row - panels
    helper = last_root + 1

    def columns(c):
        return pl.ds(pl.multiple_of(c * CHUNK, CHUNK), CHUNK)

    def y_copy(p, c, h, sems, step):
        block = y.at[p, c, h * piece : (h + 1) * piece]
        return pltpu.make_async_remote_copy(
            src_ref=block, dst_ref=block, send_sem=sems.at[p], recv_sem=recv_sem.at[p, c, h],
            device_id={"row": lax.rem(row + step, n_row)}, device_id_type=MESH,
        )

    def down(p, c, h):
        return y_copy(p, c, h, down_sem, n_row - 1)

    def up(p, c, h):
        return y_copy(p, c, h, up_sem, 1)

    own_part = pl.ds(pl.multiple_of(col * part, part), part)

    def panel_part(n, step):
        return pltpu.make_async_remote_copy(
            src_ref=pan_hbm.at[:n, own_part, tail:], dst_ref=far_pan.at[:n, own_part],
            send_sem=fp_send, recv_sem=fp_recv,
            device_id={"row": lax.rem(row + step, n_row)}, device_id_type=MESH,
        )

    def panel_share(n, step):
        return pltpu.make_async_remote_copy(
            src_ref=far_pan.at[:n, own_part], dst_ref=far_pan.at[:n, own_part],
            send_sem=ag_send, recv_sem=ag_recv,
            device_id={"col": lax.rem(col + step, n_col)}, device_id_type=MESH,
        )

    def panel_shares(n):
        others = far_pan.at[:n, : (n_col - 1) * part]
        return pltpu.make_async_remote_copy(
            src_ref=others, dst_ref=others, send_sem=ag_send, recv_sem=ag_recv,
            device_id={"col": lax.rem(col + 1, n_col)}, device_id_type=MESH,
        )

    def far_rows(c, step):
        return pltpu.make_async_remote_copy(
            src_ref=cot_hbm.at[tail:, columns(c)], dst_ref=far_own.at[c], send_sem=fo_send, recv_sem=fo_recv.at[c],
            device_id={"row": lax.rem(row + step, n_row)}, device_id_type=MESH,
        )

    def late_rows():
        return pltpu.make_async_remote_copy(
            src_ref=wht_hbm.at[:, columns(LATE)], dst_ref=late_w, send_sem=lw_send, recv_sem=lw_recv,
            device_id={"row": lax.rem(row + 1, n_row)}, device_id_type=MESH,
        )

    def late_result():
        return pltpu.make_async_remote_copy(
            src_ref=late_out, dst_ref=late_in, send_sem=lr_send, recv_sem=lr_recv,
            device_id={"row": lax.rem(row + n_row - 1, n_row)}, device_id_type=MESH,
        )

    def group(g):
        return slice(0, blocks - 1) if g == 0 else slice(blocks - 1, blocks)

    def pair_copy(p, m, g):
        place = (2 * m + 1 - core) * part
        return pltpu.make_async_remote_copy(
            src_ref=grad.at[p, group(g), pl.ds(pl.multiple_of(place, part), part)], dst_ref=rs_a.at[p, m, group(g)],
            send_sem=a_send.at[p, g], recv_sem=a_recv.at[p, g],
            device_id={"col": 2 * chip + 1 - core}, device_id_type=MESH,
        )

    def chip_copy(p, j, g):
        peer = lax.rem(chip + j, chips)
        return pltpu.make_async_remote_copy(
            src_ref=rs_a.at[p, peer, group(g)], dst_ref=rs_b.at[p, j, group(g)],
            send_sem=b_send.at[p, g], recv_sem=b_recv.at[p, g],
            device_id={"col": 2 * peer + core}, device_id_type=MESH,
        )

    def pair_all(p, g):
        return pltpu.make_async_remote_copy(
            src_ref=rs_a.at[p, :, group(g)], dst_ref=rs_a.at[p, :, group(g)],
            send_sem=a_send.at[p, g], recv_sem=a_recv.at[p, g],
            device_id={"col": 2 * chip + 1 - core}, device_id_type=MESH,
        )

    def chip_all(p, g):
        return pltpu.make_async_remote_copy(
            src_ref=rs_b.at[p, 1:, group(g)], dst_ref=rs_b.at[p, 1:, group(g)],
            send_sem=b_send.at[p, g], recv_sem=b_recv.at[p, g],
            device_id={"col": 2 * lax.rem(chip + 1, chips) + core}, device_id_type=MESH,
        )

    def y_all(p, first, sems, step):
        return pltpu.make_async_remote_copy(
            src_ref=y.at[p, first:], dst_ref=y.at[p, first:], send_sem=sems.at[p], recv_sem=recv_sem.at[p, 0, 0],
            device_id={"row": lax.rem(row + step, n_row)}, device_id_type=MESH,
        )

    def own_all():
        return pltpu.make_async_remote_copy(
            src_ref=far_own, dst_ref=far_own, send_sem=fo_send, recv_sem=fo_recv.at[0],
            device_id={"row": lax.rem(row + 1, n_row)}, device_id_type=MESH,
        )

    def groups(p, act):
        act(0)

        @pl.when((row <= n_row - 1 - p) | (p >= panels))
        def _():
            act(1)

    def lower(p):
        inner = lax.broadcasted_iota(jnp.int32, (width, width), 0)
        within = lax.broadcasted_iota(jnp.int32, (width, width), 1)
        grad[p, blocks - 1] = jnp.where(inner >= within, grad[p, blocks - 1], 0.0)

    def pair_start(p):
        @pl.when(row == n_row - 1 - p)
        def _():
            lower(p)

        def act(g):
            for m in range(chips):
                pair_copy(p, m, g).start()

        groups(p, act)

    def chip_start(p):
        def act(g):
            pair_all(p, g).wait_recv()
            for m in range(chips):
                place = pl.multiple_of((2 * m + core) * part, part)
                rs_a[p, m, group(g)] += grad[p, group(g), pl.ds(place, part)]
            for j in range(1, chips):
                chip_copy(p, j, g).start()

        groups(p, act)

    def total(p, b):
        value = rs_a[p, chip, b]
        for j in range(1, chips):
            value = value + rs_b[p, j, b]
        return value

    def finish(p):
        def act(g):
            chip_all(p, g).wait_recv()
            for b in range(blocks)[group(g)]:
                out_ref[p, :, b * width : (b + 1) * width] = total(p, b)

        out_ref[p, :, tail:] = jnp.zeros((part, width), F32)
        groups(p, act)

    def late_work():
        late_rows().wait_recv()
        yq = split(y[last, LATE])
        for b in range(blocks):
            grad[panels, b] = -product(yq, split(late_w[b * width : (b + 1) * width]), NT)
        lower(panels)
        pair_start(panels)

    def late_finish():
        for g in range(2):
            chip_all(panels, g).wait_recv()
        for b in range(blocks):
            late_out[:, b * width : (b + 1) * width] = total(panels, b)
        late_result().start()

    def solve(p, c, own):
        y[p, c] = product((dth[p], dtl[p]), split(own), NN)

    def inverse(p):
        hi, lo = split(diag_ref[p].T)
        dth[p] = hi
        dtl[p] = lo

    def receive(p, c):
        root = n_row - 1 - p
        source = row == root
        if p == last:
            source = source | (row == helper)
        if p == last - 1:
            source = source | ((row == last_root) & ((c == RAW[0]) | (c == RAW[1])))
        if p == 1:
            source = source | (row == n_row - 1)
        for h in range(PIECES):
            @pl.when(jnp.logical_not(source))
            def _():
                y_copy(p, c, h, down_sem, n_row - 1).wait_recv()

            @pl.when(jnp.logical_not(source) & (row > root) & (row < n_row - 1))
            def _():
                up(p, c, h).start()

            @pl.when((row > 0) & (row < root))
            def _():
                down(p, c, h).start()

    def send(p, c, way):
        for h in range(PIECES):
            way(p, c, h).start()

    def tail_update(p, c):
        res_ref[tail:, columns(c)] -= product((pth[p, tail:], ptl[p, tail:]), split(y[p, c]), NN)

    def keep(p, c):
        @pl.when(row == n_row - 1 - p)
        def _():
            res_ref[tail:, columns(c)] = y[p, c]

    def grad_work(q, c):
        yq = split(y[q, c])
        for b in range(blocks):
            at = slice(b * width, (b + 1) * width)
            grad[q, b] -= product(yq, (wh[c, at], wl[c, at]), NT)

    def res_work(q, c):
        yq = split(y[q, c])
        for b in range(blocks - 1):
            at = slice(b * width, (b + 1) * width)
            res_ref[at, columns(c)] -= product((pth[q, at], ptl[q, at]), yq, NN)

    def take_panels(n):
        panel_shares(n).wait_recv()
        for p in range(n):
            hi, lo = split(far_pan[p].T)
            fph[p] = hi
            fpl[p] = lo

    def far(q, c):
        far_rows(c, 1).wait_recv()
        own = far_own[c]
        for p in range(q):
            own = own - product((fph[p], fpl[p]), split(y[p, c]), NN)
        solve(q, c, own)

    def advance(p, c):
        root = n_row - 1 - p
        receive(p, c)

        @pl.when(row < root)
        def _():
            tail_update(p, c)

            @pl.when(row == root - 1)
            def _():
                solve(p + 1, c, res_ref[tail:, columns(c)])
                if p + 1 < last - 1:
                    send(p + 1, c, down)

                if p > 0:
                    send(p + 1, c, up)

        keep(p, c)

    def close(c):
        receive(last - 1, c)
        tail_update(last - 1, c)
        solve(last, c, res_ref[tail:, columns(c)])

        @pl.when(row > 0)
        def _():
            send(last, c, down)

        keep(last, c)
        for q in (last, last - 1):
            grad_work(q, c)
            res_work(q, c)

    barrier = pltpu.get_barrier_semaphore()
    for step in (1, n_row - 1):
        pl.semaphore_signal(barrier, inc=1, device_id={"row": lax.rem(row + step, n_row)}, device_id_type=MESH)
    for step in range(1, n_col):
        pl.semaphore_signal(barrier, inc=1, device_id={"col": lax.rem(col + step, n_col)}, device_id_type=MESH)

    diag_copy = pltpu.make_async_copy(diag_hbm, diag_ref, local_sem.at[0])
    tail_copy = pltpu.make_async_copy(cot_hbm.at[tail:], res_ref.at[tail:], local_sem.at[1])
    pan_copy = pltpu.make_async_copy(pan_hbm, pan_ref, local_sem.at[2])
    head_copy = pltpu.make_async_copy(cot_hbm.at[:tail], res_ref.at[:tail], local_sem.at[3])
    wht_copy = pltpu.make_async_copy(wht_hbm, wht_ref, local_sem.at[4])
    for copy in (diag_copy, tail_copy, pan_copy, wht_copy, head_copy):
        copy.start()
    diag_copy.wait()
    inverse(0)
    tail_copy.wait()
    pl.semaphore_wait(barrier, 2 + n_col - 1)

    @pl.when(row == n_row - 1)
    def _():
        @pl.loop(0, count)
        def _(c):
            solve(0, c, res_ref[tail:, columns(c)])
            send(0, c, down)

    @pl.when(row == helper)
    def _():
        panel_part(last - 1, n_row - 1).start()
        for c in RAW:
            far_rows(c, n_row - 1).start()

    @pl.when(row == n_row - 2)
    def _():
        panel_part(1, 1).start()

        @pl.loop(0, count)
        def _(c):
            far_rows(c, 1).start()

    @pl.when(row == last_root)
    def _():
        panel_part(last, 1).start()
        for c in range(LATE + 1):
            far_rows(c, 1).start()
        late_rows().start()

        @pl.loop(LATE + 1, count)
        def _(c):
            far_rows(c, 1).start()

    @pl.loop(1, panels)
    def _(p):
        inverse(p)

    pan_copy.wait()

    @pl.loop(0, panels)
    def _(p):
        for b in range(blocks):
            hi, lo = split(pan_ref[p, :, b * width : (b + 1) * width].T)
            pth[p, b * width : (b + 1) * width] = hi
            ptl[p, b * width : (b + 1) * width] = lo
        grad[p] = jnp.zeros(grad.shape[1:], F32)

    def share_panels(n, step):
        panel_part(n, step).wait_recv()
        for k in range(1, n_col):
            panel_share(n, k).start()

    @pl.when(row == helper)
    def _():
        share_panels(last, 1)

    @pl.when(row == last_root)
    def _():
        share_panels(last - 1, n_row - 1)

    @pl.when(row == n_row - 1)
    def _():
        share_panels(1, 1)

    wht_copy.wait()
    head_copy.wait()
    advance(0, 0)

    @pl.when(row == n_row - 1)
    def _():
        take_panels(1)

    spared = row == last_root

    @pl.when(row == helper)
    def _():
        take_panels(last)

    passing = (row > helper) & (row < n_row - 1)

    @pl.loop(0, count)
    def _(c):
        @pl.when(passing & (c == count - 1))
        def _():
            receive(last - 1, 0)

        hi, lo = split(wht_ref[:, columns(c)])
        wh[c] = hi
        wl[c] = lo
        grad_work(0, c)

        @pl.when(c == count - 1)
        def _():
            pair_start(0)

        res_work(0, c)

        @pl.when(c == count - 1)
        def _():
            chip_start(0)

        @pl.when(row == n_row - 1)
        def _():
            far(1, c)

        for p in range(1, last - 1):
            advance(p, c)

        @pl.when(row == helper)
        def _():
            @pl.when(c == count - 1)
            def _():
                @pl.loop(RAW[1] + 1, count)
                def _(k):
                    send(last - 1, k, down)

                send(last - 1, LATE, down)

            far(last, c)
            send(last, c, up)

            @pl.when(c == count - 1)
            def _():
                chip_start(panels)

        for q in range(1, last - 1):
            grad_work(q, c)

            @pl.when(c == count - 1)
            def _():
                pair_start(q)

            res_work(q, c)

        @pl.when(spared & (c >= 1) & (c <= 2))
        def _():
            @pl.when(c == 1)
            def _():
                take_panels(last - 1)

            r = (c - 1) * (RAW[1] - RAW[0]) + RAW[0]
            far(last - 1, r)
            close(r)

        @pl.when(c + 1 < count)
        def _():
            advance(0, c + 1)

        @pl.when(row == helper)
        def _():
            grad_work(last - 1, c)
            res_work(last - 1, c)

            @pl.when(c == LATE + 1)
            def _():
                late_work()

    for p in range(1, last - 1):
        chip_start(p)

    @pl.when(row == helper)
    def _():
        pair_start(last - 1)

    below = row < helper
    start = jnp.where(spared, len(RAW), 0)
    bulk = jnp.where(spared, count - 2, count - 1)

    @pl.loop(start, count)
    def _(t):
        c = jnp.where(below & (t > 0), jnp.where(t == count - 1, LATE, t + 1), t)

        @pl.when(t > bulk)
        def _():
            chip_start(last)

        @pl.when((row != helper) & ((t > 0) | jnp.logical_not(passing)))
        def _():
            receive(last - 1, c)

            @pl.when(below)
            def _():
                tail_update(last - 1, c)

                @pl.when(spared)
                def _():
                    solve(last, c, res_ref[tail:, columns(c)])

                    @pl.when(row > 0)
                    def _():
                        send(last, c, down)

        keep(last - 1, c)

        @pl.when(row > helper)
        def _():
            grad_work(last - 1, c)

            @pl.when(t == count - 1)
            def _():
                pair_start(last - 1)

            res_work(last - 1, c)

        receive(last, c)

        @pl.when(row < last_root)
        def _():
            tail_update(last, c)

        keep(last, c)

        @pl.when((row >= helper) & (t == count - 1))
        def _():
            chip_start(last - 1)

        @pl.when(t <= bulk)
        def _():
            grad_work(last, c)

            @pl.when(t == bulk)
            def _():
                pair_start(last)

        @pl.when(below)
        def _():
            grad_work(last - 1, c)

            @pl.when(t == count - 1)
            def _():
                pair_start(last - 1)

            res_work(last - 1, c)

        res_work(last, c)

    @pl.when(below)
    def _():
        chip_start(last - 1)

    @pl.when(jnp.logical_not(spared))
    def _():
        chip_start(last)

    for p in range(last - 1):
        finish(p)

    @pl.when(row == helper)
    def _():
        late_finish()

    finish(last)
    finish(last - 1)

    @pl.when(spared)
    def _():
        late_result().wait_recv()
        out_ref[last] += late_in[...]


    @pl.loop(0, panels)
    def _(p):
        root = n_row - 1 - p

        def act(g):
            pair_all(p, g).wait_send()
            chip_all(p, g).wait_send()

        groups(p, act)

        @pl.when((row >= root) & (row < n_row - 1) & ((p < last) | (row > last_root)) & (p != 1))
        def _():
            y_all(p, 0, up_sem, 1).wait_send()

        @pl.when((row <= root) & (row > 0) & ((p != last - 1) | (row != helper)))
        def _():
            y_all(p, 0, down_sem, n_row - 1).wait_send()

    @pl.when(row == helper)
    def _():
        y_all(last - 1, len(RAW), down_sem, n_row - 1).wait_send()
        panel_part(last - 1, n_row - 1).wait_send()
        for c in RAW:
            far_rows(c, n_row - 1).wait_send()
        panel_shares(last).wait_send()
        late_result().wait_send()
        for g in range(2):
            pair_all(panels, g).wait_send()
            chip_all(panels, g).wait_send()

    @pl.when(row == n_row - 2)
    def _():
        panel_part(1, 1).wait_send()
        own_all().wait_send()

    @pl.when(row == n_row - 1)
    def _():
        panel_shares(1).wait_send()

    @pl.when(spared)
    def _():
        panel_part(last, 1).wait_send()
        own_all().wait_send()
        panel_shares(last - 1).wait_send()
        late_rows().wait_send()


def store_kernel(res_ref, grad_ref, res_hbm, grad_hbm, sems):
    step = res_ref.shape[0] // STORES
    copies = [pltpu.make_async_copy(grad_ref, grad_hbm, sems.at[STORES])]
    for k in range(STORES):
        at = slice(k * step, (k + 1) * step)
        copies.append(pltpu.make_async_copy(res_ref.at[at], res_hbm.at[at], sems.at[k]))
    for copy in copies:
        copy.start()
    for copy in copies:
        copy.wait()


def solution(mesh):
    n_row, n_col = mesh.shape["row"], mesh.shape["col"]

    def body(cotangent, whitened, panel_rows, diag_inverse):
        rows, rhs = cotangent.shape
        panels, width = diag_inverse.shape[:2]
        assert 3 <= panels <= n_row and n_col % 2 == 0 and rhs // CHUNK > RAW[1] + 1
        count, blocks, part, chips = rhs // CHUNK, rows // width, width // n_col, n_col // 2
        anywhere = pl.BlockSpec(memory_space=pl.ANY)
        vmem = pl.BlockSpec(memory_space=pltpu.VMEM)
        hbm = pl.BlockSpec(memory_space=pltpu.HBM)
        dma = pltpu.SemaphoreType.DMA
        kept = pl.pallas_call(
            functools.partial(kernel, n_row, n_col),
            out_shape=(pltpu.VMEM((rows, rhs), F32), pltpu.VMEM((panels, part, rows), F32)),
            in_specs=[hbm] * 4,
            out_specs=(vmem, vmem),
            scratch_shapes=[
                pltpu.VMEM((rows, rhs), F32),
                pltpu.VMEM((panels, width, rows), F32),
                pltpu.VMEM((panels, width, width), F32),
                pltpu.VMEM((panels, count, width, CHUNK), F32),
                pltpu.VMEM((panels, rows, width), BF16),
                pltpu.VMEM((panels, rows, width), BF16),
                pltpu.VMEM((panels, width, width), BF16),
                pltpu.VMEM((panels, width, width), BF16),
                pltpu.VMEM((count, rows, CHUNK), BF16),
                pltpu.VMEM((count, rows, CHUNK), BF16),
                pltpu.VMEM((panels + 1, blocks, width, width), F32),
                pltpu.VMEM((panels + 1, chips, blocks, part, width), F32),
                pltpu.VMEM((panels + 1, chips, blocks, part, width), F32),
                pltpu.VMEM((panels - 1, width, width), F32),
                pltpu.VMEM((count, width, CHUNK), F32),
                pltpu.VMEM((panels - 1, width, width), BF16),
                pltpu.VMEM((panels - 1, width, width), BF16),
                pltpu.VMEM((rows, CHUNK), F32),
                pltpu.VMEM((part, rows), F32),
                pltpu.VMEM((part, rows), F32),
                dma((5,)),
                dma((panels, count, PIECES)),
                dma((panels,)),
                dma((panels,)),
                dma((panels + 1, 2)),
                dma((panels + 1, 2)),
                dma((panels + 1, 2)),
                dma((panels + 1, 2)),
                dma,
                dma,
                dma,
                dma((count,)),
                dma,
                dma,
                dma,
                dma,
                dma,
                dma,
            ],
            compiler_params=pltpu.CompilerParams(
                collective_id=0, has_side_effects=True, vmem_limit_bytes=117 * 512 * 1024
            ),
        )(cotangent, whitened, panel_rows, diag_inverse)
        return pl.pallas_call(
            store_kernel,
            out_shape=tuple(jax.ShapeDtypeStruct(k.shape, F32) for k in kept),
            in_specs=[anywhere] * 2,
            out_specs=(hbm, hbm),
            scratch_shapes=[dma((STORES + 1,))],
            compiler_params=pltpu.CompilerParams(vmem_limit_bytes=1024 * 1024),
        )(*kept)

    return jax.shard_map(
        body,
        mesh=mesh,
        in_specs=(P("row", "col"), P("row", "col"), P(None, None, "row"), P()),
        out_specs=(P("row", "col"), P(None, "col", "row")),
        check_vma=False,
    )
```

```python
import functools

import jax
import jax.numpy as jnp
from jax import lax
from jax.experimental import pallas as pl
from jax.experimental.pallas import tpu as pltpu
from jax.sharding import PartitionSpec as P

MESH = pl.DeviceIdType.MESH
CHUNK = 256
PIECES = 4
STORES = 4
RAW = (0, 2)
LATE = 1
F32 = jnp.float32
BF16 = jnp.bfloat16


def split(x):
    hi = x.astype(BF16)
    return hi, (x - hi.astype(F32)).astype(BF16)


def product(a, b, dims):
    dot = functools.partial(lax.dot_general, dimension_numbers=(dims, ((), ())), preferred_element_type=F32)
    return dot(a[0], b[0]) + (dot(a[0], b[1]) + dot(a[1], b[0]))


NN = ((1,), (0,))
NT = ((1,), (1,))


def kernel(
    n_row, n_col, cot_hbm, wht_hbm, pan_hbm, diag_hbm, res_ref, out_ref,
    wht_ref, pan_ref, diag_ref, y, pth, ptl, dth, dtl, wh, wl, grad, rs_a, rs_b,
    far_pan, far_own, fph, fpl, late_w, late_out, late_in,
    local_sem, recv_sem, down_sem, up_sem, a_send, a_recv, b_send, b_recv,
    fp_send, fp_recv, fo_send, fo_recv, ag_send, ag_recv, lw_send, lw_recv, lr_send, lr_recv,
):
    rows, rhs = res_ref.shape
    panels, width = diag_ref.shape[0], diag_ref.shape[1]
    count = rhs // CHUNK
    blocks = rows // width
    tail = rows - width
    part = width // n_col
    chips = n_col // 2
    piece = width // PIECES
    row, col = lax.axis_index("row"), lax.axis_index("col")
    core, chip = lax.rem(col, 2), col // 2
    last = panels - 1
    last_root = n_row - panels
    helper = last_root + 1

    def columns(c):
        return pl.ds(pl.multiple_of(c * CHUNK, CHUNK), CHUNK)

    def y_copy(p, c, h, sems, step):
        block = y.at[p, c, h * piece : (h + 1) * piece]
        return pltpu.make_async_remote_copy(
            src_ref=block, dst_ref=block, send_sem=sems, recv_sem=recv_sem.at[p, c, h],
            device_id={"row": lax.rem(row + step, n_row)}, device_id_type=MESH,
        )

    def down(p, c, h):
        return y_copy(p, c, h, down_sem, n_row - 1)

    def up(p, c, h):
        return y_copy(p, c, h, up_sem, 1)

    own_part = pl.ds(pl.multiple_of(col * part, part), part)

    def panel_part(n, step):
        return pltpu.make_async_remote_copy(
            src_ref=pan_hbm.at[:n, own_part, tail:], dst_ref=far_pan.at[:n, own_part],
            send_sem=fp_send, recv_sem=fp_recv,
            device_id={"row": lax.rem(row + step, n_row)}, device_id_type=MESH,
        )

    def panel_share(n, step):
        return pltpu.make_async_remote_copy(
            src_ref=far_pan.at[:n, own_part], dst_ref=far_pan.at[:n, own_part],
            send_sem=ag_send, recv_sem=ag_recv,
            device_id={"col": lax.rem(col + step, n_col)}, device_id_type=MESH,
        )

    def panel_shares(n):
        others = far_pan.at[:n, : (n_col - 1) * part]
        return pltpu.make_async_remote_copy(
            src_ref=others, dst_ref=others, send_sem=ag_send, recv_sem=ag_recv,
            device_id={"col": lax.rem(col + 1, n_col)}, device_id_type=MESH,
        )

    def far_rows(c, step):
        return pltpu.make_async_remote_copy(
            src_ref=cot_hbm.at[tail:, columns(c)], dst_ref=far_own.at[c], send_sem=fo_send, recv_sem=fo_recv.at[c],
            device_id={"row": lax.rem(row + step, n_row)}, device_id_type=MESH,
        )

    def late_rows():
        return pltpu.make_async_remote_copy(
            src_ref=wht_hbm.at[:, columns(LATE)], dst_ref=late_w, send_sem=lw_send, recv_sem=lw_recv,
            device_id={"row": lax.rem(row + 1, n_row)}, device_id_type=MESH,
        )

    def late_result():
        return pltpu.make_async_remote_copy(
            src_ref=late_out, dst_ref=late_in, send_sem=lr_send, recv_sem=lr_recv,
            device_id={"row": lax.rem(row + n_row - 1, n_row)}, device_id_type=MESH,
        )

    def group(g):
        return slice(0, blocks - 1) if g == 0 else slice(blocks - 1, blocks)

    def pair_copy(p, m, g):
        place = (2 * m + 1 - core) * part
        return pltpu.make_async_remote_copy(
            src_ref=grad.at[p, group(g), pl.ds(pl.multiple_of(place, part), part)], dst_ref=rs_a.at[p, m, group(g)],
            send_sem=a_send, recv_sem=a_recv.at[p, g],
            device_id={"col": 2 * chip + 1 - core}, device_id_type=MESH,
        )

    def chip_copy(p, j, g):
        peer = lax.rem(chip + j, chips)
        return pltpu.make_async_remote_copy(
            src_ref=rs_a.at[p, peer, group(g)], dst_ref=rs_b.at[p, j, group(g)],
            send_sem=b_send, recv_sem=b_recv.at[p, g],
            device_id={"col": 2 * peer + core}, device_id_type=MESH,
        )

    def pair_all(p, g):
        return pltpu.make_async_remote_copy(
            src_ref=rs_a.at[p, :, group(g)], dst_ref=rs_a.at[p, :, group(g)],
            send_sem=a_send, recv_sem=a_recv.at[p, g],
            device_id={"col": 2 * chip + 1 - core}, device_id_type=MESH,
        )

    def chip_all(p, g):
        return pltpu.make_async_remote_copy(
            src_ref=rs_b.at[p, 1:, group(g)], dst_ref=rs_b.at[p, 1:, group(g)],
            send_sem=b_send, recv_sem=b_recv.at[p, g],
            device_id={"col": 2 * lax.rem(chip + 1, chips) + core}, device_id_type=MESH,
        )

    def y_all(p, first, sems, step):
        return pltpu.make_async_remote_copy(
            src_ref=y.at[p, first:], dst_ref=y.at[p, first:], send_sem=sems, recv_sem=recv_sem.at[p, 0, 0],
            device_id={"row": lax.rem(row + step, n_row)}, device_id_type=MESH,
        )

    def own_all():
        return pltpu.make_async_remote_copy(
            src_ref=far_own, dst_ref=far_own, send_sem=fo_send, recv_sem=fo_recv.at[0],
            device_id={"row": lax.rem(row + 1, n_row)}, device_id_type=MESH,
        )

    def groups(p, act):
        act(0)

        @pl.when((row <= n_row - 1 - p) | (p >= panels))
        def _():
            act(1)

    def lower(p):
        inner = lax.broadcasted_iota(jnp.int32, (width, width), 0)
        within = lax.broadcasted_iota(jnp.int32, (width, width), 1)
        grad[p, blocks - 1] = jnp.where(inner >= within, grad[p, blocks - 1], 0.0)

    def pair_start(p):
        @pl.when(row == n_row - 1 - p)
        def _():
            lower(p)

        def act(g):
            for m in range(chips):
                pair_copy(p, m, g).start()

        groups(p, act)

    def chip_start(p):
        def act(g):
            pair_all(p, g).wait_recv()
            for m in range(chips):
                place = pl.multiple_of((2 * m + core) * part, part)
                rs_a[p, m, group(g)] += grad[p, group(g), pl.ds(place, part)]
            for j in range(1, chips):
                chip_copy(p, j, g).start()

        groups(p, act)

    def total(p, b):
        value = rs_a[p, chip, b]
        for j in range(1, chips):
            value = value + rs_b[p, j, b]
        return value

    def finish(p):
        def act(g):
            chip_all(p, g).wait_recv()
            for b in range(blocks)[group(g)]:
                out_ref[p, :, b * width : (b + 1) * width] = total(p, b)

        out_ref[p, :, tail:] = jnp.zeros((part, width), F32)
        groups(p, act)

    def late_work():
        late_rows().wait_recv()
        yq = split(y[last, LATE])
        for b in range(blocks):
            grad[panels, b] = -product(yq, split(late_w[b * width : (b + 1) * width]), NT)
        lower(panels)
        pair_start(panels)

    def late_finish():
        for g in range(2):
            chip_all(panels, g).wait_recv()
        for b in range(blocks):
            late_out[:, b * width : (b + 1) * width] = total(panels, b)
        late_result().start()

    def solve(p, c, own):
        y[p, c] = product((dth[p], dtl[p]), split(own), NN)

    def inverse(p):
        hi, lo = split(diag_ref[p].T)
        dth[p] = hi
        dtl[p] = lo

    def receive(p, c):
        root = n_row - 1 - p
        source = row == root
        if p == last:
            source = source | (row == helper)
        if p == last - 1:
            source = source | ((row == last_root) & ((c == RAW[0]) | (c == RAW[1])))
        if p == 1:
            source = source | (row == n_row - 1)
        for h in range(PIECES):
            @pl.when(jnp.logical_not(source))
            def _():
                y_copy(p, c, h, down_sem, n_row - 1).wait_recv()

            @pl.when(jnp.logical_not(source) & (row > root) & (row < n_row - 1))
            def _():
                up(p, c, h).start()

            @pl.when((row > 0) & (row < root))
            def _():
                down(p, c, h).start()

    def send(p, c, way):
        for h in range(PIECES):
            way(p, c, h).start()

    def tail_update(p, c):
        res_ref[tail:, columns(c)] -= product((pth[p, tail:], ptl[p, tail:]), split(y[p, c]), NN)

    def keep(p, c):
        @pl.when(row == n_row - 1 - p)
        def _():
            res_ref[tail:, columns(c)] = y[p, c]

    def grad_work(q, c):
        yq = split(y[q, c])
        for b in range(blocks):
            at = slice(b * width, (b + 1) * width)
            grad[q, b] -= product(yq, (wh[c, at], wl[c, at]), NT)

    def res_work(q, c):
        yq = split(y[q, c])
        for b in range(blocks - 1):
            at = slice(b * width, (b + 1) * width)
            res_ref[at, columns(c)] -= product((pth[q, at], ptl[q, at]), yq, NN)

    def take_panels(n):
        panel_shares(n).wait_recv()
        for p in range(n):
            hi, lo = split(far_pan[p].T)
            fph[p] = hi
            fpl[p] = lo

    def far(q, c):
        far_rows(c, 1).wait_recv()
        own = far_own[c]
        for p in range(q):
            own = own - product((fph[p], fpl[p]), split(y[p, c]), NN)
        solve(q, c, own)

    def advance(p, c):
        root = n_row - 1 - p
        receive(p, c)

        @pl.when(row < root)
        def _():
            tail_update(p, c)

            @pl.when(row == root - 1)
            def _():
                solve(p + 1, c, res_ref[tail:, columns(c)])
                if p + 1 < last - 1:
                    send(p + 1, c, down)

                if p > 0:
                    send(p + 1, c, up)

        keep(p, c)

    def close(c):
        receive(last - 1, c)
        tail_update(last - 1, c)
        solve(last, c, res_ref[tail:, columns(c)])

        @pl.when(row > 0)
        def _():
            send(last, c, down)

        keep(last, c)
        for q in (last, last - 1):
            grad_work(q, c)
            res_work(q, c)

    barrier = pltpu.get_barrier_semaphore()
    for step in (1, n_row - 1):
        pl.semaphore_signal(barrier, inc=1, device_id={"row": lax.rem(row + step, n_row)}, device_id_type=MESH)
    for step in range(1, n_col):
        pl.semaphore_signal(barrier, inc=1, device_id={"col": lax.rem(col + step, n_col)}, device_id_type=MESH)

    diag_copy = pltpu.make_async_copy(diag_hbm, diag_ref, local_sem.at[0])
    tail_copy = pltpu.make_async_copy(cot_hbm.at[tail:], res_ref.at[tail:], local_sem.at[1])
    pan_copy = pltpu.make_async_copy(pan_hbm, pan_ref, local_sem.at[2])
    head_copy = pltpu.make_async_copy(cot_hbm.at[:tail], res_ref.at[:tail], local_sem.at[3])
    wht_copy = pltpu.make_async_copy(wht_hbm, wht_ref, local_sem.at[4])
    for copy in (diag_copy, tail_copy, pan_copy, wht_copy, head_copy):
        copy.start()
    diag_copy.wait()
    inverse(0)
    tail_copy.wait()
    pl.semaphore_wait(barrier, 2 + n_col - 1)

    @pl.when(row == n_row - 1)
    def _():
        @pl.loop(0, count)
        def _(c):
            solve(0, c, res_ref[tail:, columns(c)])
            send(0, c, down)

    @pl.when(row == helper)
    def _():
        panel_part(last - 1, n_row - 1).start()
        for c in RAW:
            far_rows(c, n_row - 1).start()

    @pl.when(row == n_row - 2)
    def _():
        panel_part(1, 1).start()

        @pl.loop(0, count)
        def _(c):
            far_rows(c, 1).start()

    @pl.when(row == last_root)
    def _():
        panel_part(last, 1).start()
        for c in range(LATE + 1):
            far_rows(c, 1).start()
        late_rows().start()

        @pl.loop(LATE + 1, count)
        def _(c):
            far_rows(c, 1).start()

    @pl.loop(1, panels)
    def _(p):
        inverse(p)

    pan_copy.wait()

    @pl.loop(0, panels)
    def _(p):
        for b in range(blocks):
            hi, lo = split(pan_ref[p, :, b * width : (b + 1) * width].T)
            pth[p, b * width : (b + 1) * width] = hi
            ptl[p, b * width : (b + 1) * width] = lo
        grad[p] = jnp.zeros(grad.shape[1:], F32)

    def share_panels(n, step):
        panel_part(n, step).wait_recv()
        for k in range(1, n_col):
            panel_share(n, k).start()

    @pl.when(row == helper)
    def _():
        share_panels(last, 1)

    @pl.when(row == last_root)
    def _():
        share_panels(last - 1, n_row - 1)

    @pl.when(row == n_row - 1)
    def _():
        share_panels(1, 1)

    wht_copy.wait()
    head_copy.wait()
    advance(0, 0)

    @pl.when(row == n_row - 1)
    def _():
        take_panels(1)

    spared = row == last_root

    @pl.when(row == helper)
    def _():
        take_panels(last)

    passing = (row > helper) & (row < n_row - 1)

    @pl.loop(0, count)
    def _(c):
        @pl.when(passing & (c == count - 1))
        def _():
            receive(last - 1, 0)

        hi, lo = split(wht_ref[:, columns(c)])
        wh[c] = hi
        wl[c] = lo
        grad_work(0, c)

        @pl.when(c == count - 1)
        def _():
            pair_start(0)

        res_work(0, c)

        @pl.when(c == count - 1)
        def _():
            chip_start(0)

        @pl.when(row == n_row - 1)
        def _():
            far(1, c)

        for p in range(1, last - 1):
            advance(p, c)

        @pl.when(row == helper)
        def _():
            @pl.when(c == count - 1)
            def _():
                @pl.loop(RAW[1] + 1, count)
                def _(k):
                    send(last - 1, k, down)

                send(last - 1, LATE, down)

            far(last, c)
            send(last, c, up)

            @pl.when(c == count - 1)
            def _():
                chip_start(panels)

        for q in range(1, last - 1):
            grad_work(q, c)

            @pl.when(c == count - 1)
            def _():
                pair_start(q)

            res_work(q, c)

        @pl.when(spared & (c >= 1) & (c <= 2))
        def _():
            @pl.when(c == 1)
            def _():
                take_panels(last - 1)

            r = (c - 1) * (RAW[1] - RAW[0]) + RAW[0]
            far(last - 1, r)
            close(r)

        @pl.when(c + 1 < count)
        def _():
            advance(0, c + 1)

        @pl.when(row == helper)
        def _():
            grad_work(last - 1, c)
            res_work(last - 1, c)

            @pl.when(c == LATE + 1)
            def _():
                late_work()

    for p in range(1, last - 1):
        chip_start(p)

    @pl.when(row == helper)
    def _():
        pair_start(last - 1)

    below = row < helper
    start = jnp.where(spared, len(RAW), 0)
    bulk = jnp.where(spared, count - 2, count - 1)

    @pl.loop(start, count)
    def _(t):
        c = jnp.where(below & (t > 0), jnp.where(t == count - 1, LATE, t + 1), t)

        @pl.when((row != helper) & ((t > 0) | jnp.logical_not(passing)))
        def _():
            receive(last - 1, c)

            @pl.when(t > bulk)
            def _():
                grad_work(last - 1, c)
                pair_start(last - 1)

            @pl.when(below)
            def _():
                tail_update(last - 1, c)

                @pl.when(spared)
                def _():
                    solve(last, c, res_ref[tail:, columns(c)])

                    @pl.when(row > 0)
                    def _():
                        send(last, c, down)

        keep(last - 1, c)

        @pl.when(row > helper)
        def _():
            grad_work(last - 1, c)

            @pl.when(t == count - 1)
            def _():
                pair_start(last - 1)

            res_work(last - 1, c)

            @pl.when((row == n_row - 1) & (t == count - 1))
            def _():
                chip_start(last - 1)

        receive(last, c)

        @pl.when(row < last_root)
        def _():
            tail_update(last, c)

        keep(last, c)

        @pl.when(((row >= helper) & (row < n_row - 1) & (t == count - 1)) | (t > bulk))
        def _():
            chip_start(last - 1)

        @pl.when(t <= bulk)
        def _():
            grad_work(last, c)

            @pl.when(t == bulk)
            def _():
                pair_start(last)

        @pl.when(below & (t <= bulk))
        def _():
            grad_work(last - 1, c)

            @pl.when(t == count - 1)
            def _():
                pair_start(last - 1)

            @pl.when(spared & (t == bulk))
            def _():
                chip_start(last)

        @pl.when(below)
        def _():
            res_work(last - 1, c)

        res_work(last, c)

    @pl.when(row < last_root)
    def _():
        chip_start(last - 1)

    @pl.when(jnp.logical_not(spared))
    def _():
        chip_start(last)

    for p in range(last - 1):
        finish(p)

    @pl.when(row == helper)
    def _():
        late_finish()

    finish(last)
    finish(last - 1)

    @pl.when(spared)
    def _():
        late_result().wait_recv()
        out_ref[last] += late_in[...]


    @pl.loop(0, panels)
    def _(p):
        root = n_row - 1 - p

        def act(g):
            pair_all(p, g).wait_send()
            chip_all(p, g).wait_send()

        groups(p, act)

        @pl.when((row >= root) & (row < n_row - 1) & ((p < last) | (row > last_root)) & (p != 1))
        def _():
            y_all(p, 0, up_sem, 1).wait_send()

        @pl.when((row <= root) & (row > 0) & ((p != last - 1) | (row != helper)))
        def _():
            y_all(p, 0, down_sem, n_row - 1).wait_send()

    @pl.when(row == helper)
    def _():
        y_all(last - 1, len(RAW), down_sem, n_row - 1).wait_send()
        panel_part(last - 1, n_row - 1).wait_send()
        for c in RAW:
            far_rows(c, n_row - 1).wait_send()
        panel_shares(last).wait_send()
        late_result().wait_send()
        for g in range(2):
            pair_all(panels, g).wait_send()
            chip_all(panels, g).wait_send()

    @pl.when(row == n_row - 2)
    def _():
        panel_part(1, 1).wait_send()
        own_all().wait_send()

    @pl.when(row == n_row - 1)
    def _():
        panel_shares(1).wait_send()

    @pl.when(spared)
    def _():
        panel_part(last, 1).wait_send()
        own_all().wait_send()
        panel_shares(last - 1).wait_send()
        late_rows().wait_send()


def store_kernel(res_ref, grad_ref, res_hbm, grad_hbm, sems):
    step = res_ref.shape[0] // STORES
    copies = [pltpu.make_async_copy(grad_ref, grad_hbm, sems.at[STORES])]
    for k in range(STORES):
        at = slice(k * step, (k + 1) * step)
        copies.append(pltpu.make_async_copy(res_ref.at[at], res_hbm.at[at], sems.at[k]))
    for copy in copies:
        copy.start()
    for copy in copies:
        copy.wait()


def solution(mesh):
    n_row, n_col = mesh.shape["row"], mesh.shape["col"]

    def body(cotangent, whitened, panel_rows, diag_inverse):
        rows, rhs = cotangent.shape
        panels, width = diag_inverse.shape[:2]
        assert 3 <= panels <= n_row and n_col % 2 == 0 and rhs // CHUNK > RAW[1] + 1
        count, blocks, part, chips = rhs // CHUNK, rows // width, width // n_col, n_col // 2
        anywhere = pl.BlockSpec(memory_space=pl.ANY)
        vmem = pl.BlockSpec(memory_space=pltpu.VMEM)
        hbm = pl.BlockSpec(memory_space=pltpu.HBM)
        dma = pltpu.SemaphoreType.DMA
        kept = pl.pallas_call(
            functools.partial(kernel, n_row, n_col),
            out_shape=(pltpu.VMEM((rows, rhs), F32), pltpu.VMEM((panels, part, rows), F32)),
            in_specs=[hbm] * 4,
            out_specs=(vmem, vmem),
            scratch_shapes=[
                pltpu.VMEM((rows, rhs), F32),
                pltpu.VMEM((panels, width, rows), F32),
                pltpu.VMEM((panels, width, width), F32),
                pltpu.VMEM((panels, count, width, CHUNK), F32),
                pltpu.VMEM((panels, rows, width), BF16),
                pltpu.VMEM((panels, rows, width), BF16),
                pltpu.VMEM((panels, width, width), BF16),
                pltpu.VMEM((panels, width, width), BF16),
                pltpu.VMEM((count, rows, CHUNK), BF16),
                pltpu.VMEM((count, rows, CHUNK), BF16),
                pltpu.VMEM((panels + 1, blocks, width, width), F32),
                pltpu.VMEM((panels + 1, chips, blocks, part, width), F32),
                pltpu.VMEM((panels + 1, chips, blocks, part, width), F32),
                pltpu.VMEM((panels - 1, width, width), F32),
                pltpu.VMEM((count, width, CHUNK), F32),
                pltpu.VMEM((panels - 1, width, width), BF16),
                pltpu.VMEM((panels - 1, width, width), BF16),
                pltpu.VMEM((rows, CHUNK), F32),
                pltpu.VMEM((part, rows), F32),
                pltpu.VMEM((part, rows), F32),
                dma((5,)),
                dma((panels, count, PIECES)),
                dma,
                dma,
                dma,
                dma((panels + 1, 2)),
                dma,
                dma((panels + 1, 2)),
                dma,
                dma,
                dma,
                dma((count,)),
                dma,
                dma,
                dma,
                dma,
                dma,
                dma,
            ],
            compiler_params=pltpu.CompilerParams(
                collective_id=0, has_side_effects=True, vmem_limit_bytes=117 * 512 * 1024
            ),
        )(cotangent, whitened, panel_rows, diag_inverse)
        return pl.pallas_call(
            store_kernel,
            out_shape=tuple(jax.ShapeDtypeStruct(k.shape, F32) for k in kept),
            in_specs=[anywhere] * 2,
            out_specs=(hbm, hbm),
            scratch_shapes=[dma((STORES + 1,))],
            compiler_params=pltpu.CompilerParams(vmem_limit_bytes=1024 * 1024),
        )(*kept)

    return jax.shard_map(
        body,
        mesh=mesh,
        in_specs=(P("row", "col"), P("row", "col"), P(None, None, "row"), P()),
        out_specs=(P("row", "col"), P(None, "col", "row")),
        check_vma=False,
    )
```

```python
import functools

import jax
import jax.numpy as jnp
from jax import lax
from jax.experimental import pallas as pl
from jax.experimental.pallas import tpu as pltpu
from jax.sharding import PartitionSpec as P

MESH = pl.DeviceIdType.MESH
CHUNK = 256
PIECES = (4, 4, 2, 4)
STORES = 4
RAW = (0, 2)
LATE = 1
F32 = jnp.float32
BF16 = jnp.bfloat16


def split(x):
    hi = x.astype(BF16)
    return hi, (x - hi.astype(F32)).astype(BF16)


def product(a, b, dims):
    dot = functools.partial(lax.dot_general, dimension_numbers=(dims, ((), ())), preferred_element_type=F32)
    return dot(a[0], b[0]) + (dot(a[0], b[1]) + dot(a[1], b[0]))


NN = ((1,), (0,))
NT = ((1,), (1,))


def kernel(
    n_row, n_col, cot_hbm, wht_hbm, pan_hbm, diag_hbm, res_ref, out_ref,
    wht_ref, pan_ref, diag_ref, y, pth, ptl, dth, dtl, wh, wl, grad, rs_a, rs_b,
    far_pan, far_own, fph, fpl, late_w, late_c, late_out, late_in,
    local_sem, recv_sem, down_sem, up_sem, a_send, a_recv, b_send, b_recv,
    misc_send, fp_recv, fo_recv, ag_recv, lw_recv, lc_recv, lr_recv,
):
    rows, rhs = res_ref.shape
    panels, width = diag_ref.shape[0], diag_ref.shape[1]
    count = rhs // CHUNK
    blocks = rows // width
    tail = rows - width
    part = width // n_col
    chips = n_col // 2
    offset = [sum(PIECES[:p]) for p in range(panels)]
    row, col = lax.axis_index("row"), lax.axis_index("col")
    core, chip = lax.rem(col, 2), col // 2
    last = panels - 1
    last_root = n_row - panels
    helper = last_root + 1
    spared = row == last_root
    lane = width // 2
    lanes = 2 * blocks
    late, corner = panels, panels + 1

    def columns(c):
        return pl.ds(pl.multiple_of(c * CHUNK, CHUNK), CHUNK)

    def y_copy(p, c, h, sems, step):
        piece = width // PIECES[p]
        block = y.at[p, c, h * piece : (h + 1) * piece]
        return pltpu.make_async_remote_copy(
            src_ref=block, dst_ref=block, send_sem=sems, recv_sem=recv_sem.at[c, offset[p] + h],
            device_id={"row": lax.rem(row + step, n_row)}, device_id_type=MESH,
        )

    def down(p, c, h):
        return y_copy(p, c, h, down_sem, n_row - 1)

    def up(p, c, h):
        return y_copy(p, c, h, up_sem, 1)

    own_part = pl.ds(pl.multiple_of(col * part, part), part)

    def panel_part(n, step):
        return pltpu.make_async_remote_copy(
            src_ref=pan_hbm.at[:n, own_part, tail:], dst_ref=far_pan.at[:n, own_part],
            send_sem=misc_send, recv_sem=fp_recv,
            device_id={"row": lax.rem(row + step, n_row)}, device_id_type=MESH,
        )

    def panel_share(n, step):
        return pltpu.make_async_remote_copy(
            src_ref=far_pan.at[:n, own_part], dst_ref=far_pan.at[:n, own_part],
            send_sem=misc_send, recv_sem=ag_recv,
            device_id={"col": lax.rem(col + step, n_col)}, device_id_type=MESH,
        )

    def panel_shares(n):
        others = far_pan.at[:n, : (n_col - 1) * part]
        return pltpu.make_async_remote_copy(
            src_ref=others, dst_ref=others, send_sem=misc_send, recv_sem=ag_recv,
            device_id={"col": lax.rem(col + 1, n_col)}, device_id_type=MESH,
        )

    def far_rows(c, step):
        return pltpu.make_async_remote_copy(
            src_ref=cot_hbm.at[tail:, columns(c)], dst_ref=far_own.at[c], send_sem=misc_send, recv_sem=fo_recv.at[c],
            device_id={"row": lax.rem(row + step, n_row)}, device_id_type=MESH,
        )

    def late_rows():
        return pltpu.make_async_remote_copy(
            src_ref=wht_hbm.at[:, columns(LATE)], dst_ref=late_w, send_sem=misc_send, recv_sem=lw_recv,
            device_id={"row": lax.rem(row + 1, n_row)}, device_id_type=MESH,
        )

    def corner_rows():
        return pltpu.make_async_remote_copy(
            src_ref=wht_hbm.at[:lane], dst_ref=late_c, send_sem=misc_send, recv_sem=lc_recv,
            device_id={"row": lax.rem(row + 1, n_row)}, device_id_type=MESH,
        )

    def late_result():
        return pltpu.make_async_remote_copy(
            src_ref=late_out, dst_ref=late_in, send_sem=misc_send, recv_sem=lr_recv,
            device_id={"row": lax.rem(row + n_row - 1, n_row)}, device_id_type=MESH,
        )

    def group(g):
        return (slice(0, lanes - 2), slice(1, 4), slice(4, lanes - 2), slice(lanes - 2, lanes))[g]

    def pair_copy(p, m, g):
        place = (2 * m + 1 - core) * part
        return pltpu.make_async_remote_copy(
            src_ref=grad.at[p, group(g), pl.ds(pl.multiple_of(place, part), part)], dst_ref=rs_a.at[p, m, group(g)],
            send_sem=a_send, recv_sem=a_recv.at[p, g],
            device_id={"col": 2 * chip + 1 - core}, device_id_type=MESH,
        )

    def chip_copy(p, j, g):
        peer = lax.rem(chip + j, chips)
        return pltpu.make_async_remote_copy(
            src_ref=rs_a.at[p, peer, group(g)], dst_ref=rs_b.at[p, j, group(g)],
            send_sem=b_send, recv_sem=b_recv.at[p, g],
            device_id={"col": 2 * peer + core}, device_id_type=MESH,
        )

    def pair_all(p, g):
        return pltpu.make_async_remote_copy(
            src_ref=rs_a.at[p, :, group(g)], dst_ref=rs_a.at[p, :, group(g)],
            send_sem=a_send, recv_sem=a_recv.at[p, g],
            device_id={"col": 2 * chip + 1 - core}, device_id_type=MESH,
        )

    def chip_all(p, g):
        return pltpu.make_async_remote_copy(
            src_ref=rs_b.at[p, 1:, group(g)], dst_ref=rs_b.at[p, 1:, group(g)],
            send_sem=b_send, recv_sem=b_recv.at[p, g],
            device_id={"col": 2 * lax.rem(chip + 1, chips) + core}, device_id_type=MESH,
        )

    def y_all(p, first, sems, step):
        return pltpu.make_async_remote_copy(
            src_ref=y.at[p, first:], dst_ref=y.at[p, first:], send_sem=sems, recv_sem=recv_sem.at[0, 0],
            device_id={"row": lax.rem(row + step, n_row)}, device_id_type=MESH,
        )

    def own_all():
        return pltpu.make_async_remote_copy(
            src_ref=far_own, dst_ref=far_own, send_sem=misc_send, recv_sem=fo_recv.at[0],
            device_id={"row": lax.rem(row + 1, n_row)}, device_id_type=MESH,
        )

    def groups(p, act):
        if isinstance(p, int) and p >= panels:
            for g in (1, 2, 3) if p == late else (3,):
                act(g)
            return

        short = spared & (p >= last - 1)

        @pl.when(jnp.logical_not(short))
        def _():
            act(0)

        @pl.when(short)
        def _():
            act(1)
            act(2)

        @pl.when(row <= n_row - 1 - p)
        def _():
            act(3)

    def lower(p):
        inner = lax.broadcasted_iota(jnp.int32, (width, lane), 0)
        within = lax.broadcasted_iota(jnp.int32, (width, lane), 1)
        for k in range(2):
            at = lanes - 2 + k
            grad[p, at] = jnp.where(inner >= within + k * lane, grad[p, at], 0.0)

    def pair_group(p, g):
        for m in range(chips):
            pair_copy(p, m, g).start()

    def pair_start(p):
        if p < panels:
            @pl.when(row == n_row - 1 - p)
            def _():
                lower(p)

        groups(p, functools.partial(pair_group, p))

    def chip_start(p):
        def act(g):
            pair_all(p, g).wait_recv()
            for m in range(chips):
                place = pl.multiple_of((2 * m + core) * part, part)
                rs_a[p, m, group(g)] += grad[p, group(g), pl.ds(place, part)]
            for j in range(1, chips):
                chip_copy(p, j, g).start()

        groups(p, act)

    def total(p, b):
        value = rs_a[p, chip, b]
        for j in range(1, chips):
            value = value + rs_b[p, j, b]
        return value

    def finish(p):
        def act(g):
            chip_all(p, g).wait_recv()
            for b in range(lanes)[group(g)]:
                out_ref[p, :, b * lane : (b + 1) * lane] = total(p, b)

        out_ref[p, :, tail:] = jnp.zeros((part, width), F32)
        groups(p, act)

    def late_work():
        late_rows().wait_recv()
        yq = split(y[last, LATE])
        for b in range(blocks):
            value = product(yq, split(late_w[b * width : (b + 1) * width]), NT)
            grad[late, 2 * b] = -value[:, :lane]
            grad[late, 2 * b + 1] = -value[:, lane:]
        lower(late)
        pair_start(late)

    def corner_work():
        corner_rows().wait_recv()
        for k in range(2):
            value = None
            for c in range(count):
                term = product(split(y[last - 1 + k, c]), split(late_c[:, c * CHUNK : (c + 1) * CHUNK]), NT)
                value = term if value is None else value + term
            grad[corner, lanes - 2 + k] = -value
        pair_start(corner)

    def late_finish():
        def act(p, shift, g):
            chip_all(p, g).wait_recv()
            for b in range(lanes)[group(g)]:
                late_out[:, (b + shift) * lane : (b + shift + 1) * lane] = total(p, b)

        late_out[:, :lane] = jnp.zeros((part, lane), F32)
        groups(late, functools.partial(act, late, 0))
        groups(corner, functools.partial(act, corner, 2))
        late_result().start()

    def solve(p, c, own):
        y[p, c] = product((dth[p], dtl[p]), split(own), NN)

    def inverse(p):
        hi, lo = split(diag_ref[p].T)
        dth[p] = hi
        dtl[p] = lo

    def receive(p, c):
        root = n_row - 1 - p
        source = row == root
        if p == last:
            source = source | (row == helper)
        if p == last - 1:
            source = source | ((row == last_root) & ((c == RAW[0]) | (c == RAW[1])))
        if p == 1:
            source = source | (row == n_row - 1)
        for h in range(PIECES[p]):
            @pl.when(jnp.logical_not(source))
            def _():
                y_copy(p, c, h, down_sem, n_row - 1).wait_recv()

            @pl.when(jnp.logical_not(source) & (row > root) & (row < n_row - 1))
            def _():
                up(p, c, h).start()

            @pl.when((row > 0) & (row < root))
            def _():
                down(p, c, h).start()

    def send(p, c, way):
        for h in range(PIECES[p]):
            way(p, c, h).start()

    def tail_update(p, c):
        res_ref[tail:, columns(c)] -= product((pth[p, tail:], ptl[p, tail:]), split(y[p, c]), NN)

    def keep(p, c):
        @pl.when(row == n_row - 1 - p)
        def _():
            res_ref[tail:, columns(c)] = y[p, c]

    def grad_block(q, c, yq, b):
        at = slice(b * width, (b + 1) * width)
        value = product(yq, (wh[c, at], wl[c, at]), NT)
        grad[q, 2 * b] -= value[:, :lane]
        grad[q, 2 * b + 1] -= value[:, lane:]

    def grad_work(q, c):
        yq = split(y[q, c])
        for b in range(blocks):
            grad_block(q, c, yq, b)

    def grad_last(c):
        yq = split(y[last - 1, c])
        for b in range(blocks):
            grad_block(last - 1, c, yq, b)
            for g in range(1, 4):
                if group(g).stop == 2 * b + 2:
                    pair_group(last - 1, g)

    def res_work(q, c):
        yq = split(y[q, c])
        for b in range(blocks - 1):
            at = slice(b * width, (b + 1) * width)
            res_ref[at, columns(c)] -= product((pth[q, at], ptl[q, at]), yq, NN)

    def take_panels(n):
        panel_shares(n).wait_recv()
        for p in range(n):
            hi, lo = split(far_pan[p].T)
            fph[p] = hi
            fpl[p] = lo

    def far(q, c):
        far_rows(c, 1).wait_recv()
        own = far_own[c]
        for p in range(q):
            own = own - product((fph[p], fpl[p]), split(y[p, c]), NN)
        solve(q, c, own)

    def advance(p, c):
        root = n_row - 1 - p
        receive(p, c)

        @pl.when(row < root)
        def _():
            tail_update(p, c)

            @pl.when(row == root - 1)
            def _():
                solve(p + 1, c, res_ref[tail:, columns(c)])
                if p + 1 < last - 1:
                    send(p + 1, c, down)

                if p > 0:
                    send(p + 1, c, up)

        keep(p, c)

    def close(c):
        receive(last - 1, c)
        tail_update(last - 1, c)
        solve(last, c, res_ref[tail:, columns(c)])

        @pl.when(row > 0)
        def _():
            send(last, c, down)

        keep(last, c)
        for q in (last, last - 1):
            grad_work(q, c)
            res_work(q, c)

    barrier = pltpu.get_barrier_semaphore()
    for step in (1, n_row - 1):
        pl.semaphore_signal(barrier, inc=1, device_id={"row": lax.rem(row + step, n_row)}, device_id_type=MESH)
    for step in range(1, n_col):
        pl.semaphore_signal(barrier, inc=1, device_id={"col": lax.rem(col + step, n_col)}, device_id_type=MESH)

    diag_copy = pltpu.make_async_copy(diag_hbm, diag_ref, local_sem.at[0])
    tail_copy = pltpu.make_async_copy(cot_hbm.at[tail:], res_ref.at[tail:], local_sem.at[1])
    pan_copy = pltpu.make_async_copy(pan_hbm, pan_ref, local_sem.at[2])
    head_copy = pltpu.make_async_copy(cot_hbm.at[:tail], res_ref.at[:tail], local_sem.at[3])
    wht_copy = pltpu.make_async_copy(wht_hbm, wht_ref, local_sem.at[4])
    for copy in (diag_copy, tail_copy, pan_copy, wht_copy, head_copy):
        copy.start()
    pl.semaphore_wait(barrier, 2 + n_col - 1)

    @pl.when(row == helper)
    def _():
        panel_part(last - 1, n_row - 1).start()
        for c in RAW:
            far_rows(c, n_row - 1).start()

    @pl.when(row == n_row - 2)
    def _():
        panel_part(1, 1).start()

        @pl.loop(0, count)
        def _(c):
            far_rows(c, 1).start()

    @pl.when(row == last_root)
    def _():
        panel_part(last, 1).start()
        for c in range(LATE + 1):
            far_rows(c, 1).start()
        late_rows().start()

        @pl.loop(LATE + 1, count)
        def _(c):
            far_rows(c, 1).start()

        corner_rows().start()

    diag_copy.wait()
    inverse(0)
    tail_copy.wait()

    @pl.when(row == n_row - 1)
    def _():
        @pl.loop(0, count)
        def _(c):
            solve(0, c, res_ref[tail:, columns(c)])
            send(0, c, down)

    @pl.loop(1, panels)
    def _(p):
        inverse(p)

    pan_copy.wait()

    @pl.loop(0, panels)
    def _(p):
        for b in range(blocks):
            hi, lo = split(pan_ref[p, :, b * width : (b + 1) * width].T)
            pth[p, b * width : (b + 1) * width] = hi
            ptl[p, b * width : (b + 1) * width] = lo
        grad[p] = jnp.zeros(grad.shape[1:], F32)

    def share_panels(n, step):
        panel_part(n, step).wait_recv()
        for k in range(1, n_col):
            panel_share(n, k).start()

    @pl.when(row == helper)
    def _():
        share_panels(last, 1)

    @pl.when(row == last_root)
    def _():
        share_panels(last - 1, n_row - 1)

    @pl.when(row == n_row - 1)
    def _():
        share_panels(1, 1)

    wht_copy.wait()
    head_copy.wait()
    advance(0, 0)

    @pl.when(row == n_row - 1)
    def _():
        take_panels(1)

    @pl.when(row == helper)
    def _():
        take_panels(last)

    passing = (row > helper) & (row < n_row - 1)

    @pl.loop(0, count)
    def _(c):
        @pl.when(passing & (c == count - 1))
        def _():
            receive(last - 1, 0)

        hi, lo = split(wht_ref[:, columns(c)])
        wh[c] = hi
        wl[c] = lo
        grad_work(0, c)

        @pl.when(c == count - 1)
        def _():
            pair_start(0)

        res_work(0, c)

        @pl.when(c == count - 1)
        def _():
            chip_start(0)

        @pl.when(row == n_row - 1)
        def _():
            far(1, c)

        for p in range(1, last - 1):
            advance(p, c)

        @pl.when(row == helper)
        def _():
            @pl.when(c == count - 1)
            def _():
                @pl.loop(RAW[1] + 1, count)
                def _(k):
                    send(last - 1, k, down)

                send(last - 1, LATE, down)

            far(last, c)
            send(last, c, up)

            @pl.when(c == LATE + 1)
            def _():
                late_work()

        for q in range(1, last - 1):
            grad_work(q, c)

            @pl.when(c == count - 1)
            def _():
                pair_start(q)

            res_work(q, c)

        @pl.when(spared & (c >= 1) & (c <= 2))
        def _():
            @pl.when(c == 1)
            def _():
                take_panels(last - 1)

            r = (c - 1) * (RAW[1] - RAW[0]) + RAW[0]
            far(last - 1, r)
            close(r)

        @pl.when(c + 1 < count)
        def _():
            advance(0, c + 1)

        @pl.when(row == helper)
        def _():
            grad_work(last - 1, c)
            res_work(last - 1, c)

            @pl.when(c == LATE + 1)
            def _():
                chip_start(late)

    for p in range(1, last - 1):
        chip_start(p)

    @pl.when(row == helper)
    def _():
        pair_start(last - 1)

    below = row < helper
    start = jnp.where(spared, len(RAW), 0)
    bulk = jnp.where(spared, count - 2, count - 1)

    @pl.loop(start, count)
    def _(t):
        c = jnp.where(below & (t > 0), jnp.where(t == count - 1, LATE, t + 1), t)

        @pl.when((row != helper) & ((t > 0) | jnp.logical_not(passing)))
        def _():
            receive(last - 1, c)

        @pl.when((row != helper) & jnp.logical_not(spared))
        def _():
            grad_work(last - 1, c)

            @pl.when(t == count - 1)
            def _():
                pair_start(last - 1)

        @pl.when(t > bulk)
        def _():
            grad_last(c)

        @pl.when(below)
        def _():
            tail_update(last - 1, c)

            @pl.when(spared)
            def _():
                solve(last, c, res_ref[tail:, columns(c)])

                @pl.when(row > 0)
                def _():
                    send(last, c, down)

        @pl.when(t > bulk)
        def _():
            chip_start(last - 1)

        keep(last - 1, c)

        @pl.when(row > helper)
        def _():
            res_work(last - 1, c)

            @pl.when((row == n_row - 1) & (t == count - 1))
            def _():
                chip_start(last - 1)

        receive(last, c)

        @pl.when(row < last_root)
        def _():
            tail_update(last, c)

        keep(last, c)

        @pl.when((row > helper) & (row < n_row - 1) & (t == count - 1) | (row == helper) & (t == 0))
        def _():
            chip_start(last - 1)

        @pl.when(t <= bulk)
        def _():
            grad_work(last, c)

            @pl.when(t == bulk)
            def _():
                pair_start(last)

        @pl.when(spared & (t <= bulk))
        def _():
            grad_work(last - 1, c)

            @pl.when(t == bulk)
            def _():
                chip_start(last)

        @pl.when(row == helper)
        def _():
            @pl.when(t == 1)
            def _():
                corner_work()

            @pl.when(t == 2)
            def _():
                chip_start(corner)

        @pl.when(below)
        def _():
            res_work(last - 1, c)

        res_work(last, c)

    @pl.when(row < last_root)
    def _():
        chip_start(last - 1)

    @pl.when(jnp.logical_not(spared))
    def _():
        chip_start(last)

    for p in range(last - 1):
        finish(p)

    @pl.when(row == helper)
    def _():
        late_finish()

    finish(last)
    finish(last - 1)

    @pl.when(spared)
    def _():
        late_result().wait_recv()
        out_ref[last - 1, :, :lane] = late_in[:, rows : rows + lane]
        out_ref[last, :, lane:] += late_in[:, lane:rows]
        out_ref[last, :, :lane] = late_in[:, rows + lane :]


    @pl.loop(0, panels)
    def _(p):
        root = n_row - 1 - p

        def act(g):
            pair_all(p, g).wait_send()
            chip_all(p, g).wait_send()

        groups(p, act)

        @pl.when((row >= root) & (row < n_row - 1) & ((p < last) | (row > last_root)) & (p != 1))
        def _():
            y_all(p, 0, up_sem, 1).wait_send()

        @pl.when((row <= root) & (row > 0) & ((p != last - 1) | (row != helper)))
        def _():
            y_all(p, 0, down_sem, n_row - 1).wait_send()

    @pl.when(row == helper)
    def _():
        y_all(last - 1, len(RAW), down_sem, n_row - 1).wait_send()
        panel_part(last - 1, n_row - 1).wait_send()
        for c in RAW:
            far_rows(c, n_row - 1).wait_send()
        panel_shares(last).wait_send()
        late_result().wait_send()
        for p in (late, corner):
            def act(g):
                pair_all(p, g).wait_send()
                chip_all(p, g).wait_send()

            groups(p, act)

    @pl.when(row == n_row - 2)
    def _():
        panel_part(1, 1).wait_send()
        own_all().wait_send()

    @pl.when(row == n_row - 1)
    def _():
        panel_shares(1).wait_send()

    @pl.when(spared)
    def _():
        panel_part(last, 1).wait_send()
        own_all().wait_send()
        panel_shares(last - 1).wait_send()
        late_rows().wait_send()
        corner_rows().wait_send()


def store_kernel(res_ref, grad_ref, res_hbm, grad_hbm, sems):
    step = res_ref.shape[0] // STORES
    copies = [pltpu.make_async_copy(grad_ref, grad_hbm, sems.at[STORES])]
    for k in range(STORES):
        at = slice(k * step, (k + 1) * step)
        copies.append(pltpu.make_async_copy(res_ref.at[at], res_hbm.at[at], sems.at[k]))
    for copy in copies:
        copy.start()
    for copy in copies:
        copy.wait()


def solution(mesh):
    n_row, n_col = mesh.shape["row"], mesh.shape["col"]

    def body(cotangent, whitened, panel_rows, diag_inverse):
        rows, rhs = cotangent.shape
        panels, width = diag_inverse.shape[:2]
        assert panels == len(PIECES) <= n_row and n_col % 2 == 0 and rhs // CHUNK > RAW[1] + 1
        count, blocks, part, chips = rhs // CHUNK, rows // width, width // n_col, n_col // 2
        anywhere = pl.BlockSpec(memory_space=pl.ANY)
        vmem = pl.BlockSpec(memory_space=pltpu.VMEM)
        hbm = pl.BlockSpec(memory_space=pltpu.HBM)
        dma = pltpu.SemaphoreType.DMA
        kept = pl.pallas_call(
            functools.partial(kernel, n_row, n_col),
            out_shape=(pltpu.VMEM((rows, rhs), F32), pltpu.VMEM((panels, part, rows), F32)),
            in_specs=[hbm] * 4,
            out_specs=(vmem, vmem),
            scratch_shapes=[
                pltpu.VMEM((rows, rhs), F32),
                pltpu.VMEM((panels, width, rows), F32),
                pltpu.VMEM((panels, width, width), F32),
                pltpu.VMEM((panels, count, width, CHUNK), F32),
                pltpu.VMEM((panels, rows, width), BF16),
                pltpu.VMEM((panels, rows, width), BF16),
                pltpu.VMEM((panels, width, width), BF16),
                pltpu.VMEM((panels, width, width), BF16),
                pltpu.VMEM((count, rows, CHUNK), BF16),
                pltpu.VMEM((count, rows, CHUNK), BF16),
                pltpu.VMEM((panels + 2, 2 * blocks, width, width // 2), F32),
                pltpu.VMEM((panels + 2, chips, 2 * blocks, part, width // 2), F32),
                pltpu.VMEM((panels + 2, chips, 2 * blocks, part, width // 2), F32),
                pltpu.VMEM((panels - 1, width, width), F32),
                pltpu.VMEM((count, width, CHUNK), F32),
                pltpu.VMEM((panels - 1, width, width), BF16),
                pltpu.VMEM((panels - 1, width, width), BF16),
                pltpu.VMEM((rows, CHUNK), F32),
                pltpu.VMEM((width // 2, rhs), F32),
                pltpu.VMEM((part, rows + width), F32),
                pltpu.VMEM((part, rows + width), F32),
                dma((5,)),
                dma((count, sum(PIECES))),
                dma,
                dma,
                dma,
                dma((panels + 2, 4)),
                dma,
                dma((panels + 2, 4)),
                dma,
                dma,
                dma((count,)),
                dma,
                dma,
                dma,
                dma,
            ],
            compiler_params=pltpu.CompilerParams(
                collective_id=0, has_side_effects=True, vmem_limit_bytes=117 * 512 * 1024
            ),
        )(cotangent, whitened, panel_rows, diag_inverse)
        return pl.pallas_call(
            store_kernel,
            out_shape=tuple(jax.ShapeDtypeStruct(k.shape, F32) for k in kept),
            in_specs=[anywhere] * 2,
            out_specs=(hbm, hbm),
            scratch_shapes=[dma((STORES + 1,))],
            compiler_params=pltpu.CompilerParams(vmem_limit_bytes=1024 * 1024),
        )(*kept)

    return jax.shard_map(
        body,
        mesh=mesh,
        in_specs=(P("row", "col"), P("row", "col"), P(None, None, "row"), P()),
        out_specs=(P("row", "col"), P(None, "col", "row")),
        check_vma=False,
    )
```

```python
import functools

import jax
import jax.numpy as jnp
from jax import lax
from jax.experimental import pallas as pl
from jax.experimental.pallas import tpu as pltpu
from jax.sharding import PartitionSpec as P

MESH = pl.DeviceIdType.MESH
CHUNK = 256
PIECES = (4, 4, 2, 4)
STORES = 4
RAW = (0, 2)
LATE = 1
F32 = jnp.float32
BF16 = jnp.bfloat16


def split(x):
    hi = x.astype(BF16)
    return hi, (x - hi.astype(F32)).astype(BF16)


def product(a, b, dims):
    dot = functools.partial(lax.dot_general, dimension_numbers=(dims, ((), ())), preferred_element_type=F32)
    return dot(a[0], b[0]) + (dot(a[0], b[1]) + dot(a[1], b[0]))


NN = ((1,), (0,))
NT = ((1,), (1,))


def kernel(
    n_row, n_col, cot_hbm, wht_hbm, pan_hbm, diag_hbm, res_ref, out_ref,
    wht_ref, pan_ref, diag_ref, y, pth, ptl, dth, dtl, wh, wl, grad, rs_a, rs_b,
    far_pan, far_own, fph, fpl, late_w, late_c, late_out, late_in,
    local_sem, recv_sem, down_sem, up_sem, a_send, a_recv, b_send, b_recv,
    misc_send, fp_recv, fo_recv, ag_recv, lw_recv, lc_recv, lr_recv,
):
    rows, rhs = res_ref.shape
    panels, width = diag_ref.shape[0], diag_ref.shape[1]
    count = rhs // CHUNK
    blocks = rows // width
    tail = rows - width
    part = width // n_col
    chips = n_col // 2
    offset = [sum(PIECES[:p]) for p in range(panels)]
    row, col = lax.axis_index("row"), lax.axis_index("col")
    core, chip = lax.rem(col, 2), col // 2
    last = panels - 1
    last_root = n_row - panels
    helper = last_root + 1
    spared = row == last_root
    lane = width // 2
    lanes = 2 * blocks
    late, corner = panels, panels + 1

    def columns(c):
        return pl.ds(pl.multiple_of(c * CHUNK, CHUNK), CHUNK)

    def y_copy(p, c, h, sems, step):
        piece = width // PIECES[p]
        block = y.at[p, c, h * piece : (h + 1) * piece]
        return pltpu.make_async_remote_copy(
            src_ref=block, dst_ref=block, send_sem=sems, recv_sem=recv_sem.at[c, offset[p] + h],
            device_id={"row": lax.rem(row + step, n_row)}, device_id_type=MESH,
        )

    def down(p, c, h):
        return y_copy(p, c, h, down_sem, n_row - 1)

    def up(p, c, h):
        return y_copy(p, c, h, up_sem, 1)

    own_part = pl.ds(pl.multiple_of(col * part, part), part)

    def panel_part(n, step):
        return pltpu.make_async_remote_copy(
            src_ref=pan_hbm.at[:n, own_part, tail:], dst_ref=far_pan.at[:n, own_part],
            send_sem=misc_send, recv_sem=fp_recv,
            device_id={"row": lax.rem(row + step, n_row)}, device_id_type=MESH,
        )

    def panel_share(n, step):
        return pltpu.make_async_remote_copy(
            src_ref=far_pan.at[:n, own_part], dst_ref=far_pan.at[:n, own_part],
            send_sem=misc_send, recv_sem=ag_recv,
            device_id={"col": lax.rem(col + step, n_col)}, device_id_type=MESH,
        )

    def panel_shares(n):
        others = far_pan.at[:n, : (n_col - 1) * part]
        return pltpu.make_async_remote_copy(
            src_ref=others, dst_ref=others, send_sem=misc_send, recv_sem=ag_recv,
            device_id={"col": lax.rem(col + 1, n_col)}, device_id_type=MESH,
        )

    def far_rows(c, step):
        return pltpu.make_async_remote_copy(
            src_ref=cot_hbm.at[tail:, columns(c)], dst_ref=far_own.at[c], send_sem=misc_send, recv_sem=fo_recv.at[c],
            device_id={"row": lax.rem(row + step, n_row)}, device_id_type=MESH,
        )

    def late_rows():
        return pltpu.make_async_remote_copy(
            src_ref=wht_hbm.at[:, columns(LATE)], dst_ref=late_w, send_sem=misc_send, recv_sem=lw_recv,
            device_id={"row": lax.rem(row + 1, n_row)}, device_id_type=MESH,
        )

    def corner_rows():
        return pltpu.make_async_remote_copy(
            src_ref=wht_hbm.at[:lane], dst_ref=late_c, send_sem=misc_send, recv_sem=lc_recv,
            device_id={"row": lax.rem(row + 1, n_row)}, device_id_type=MESH,
        )

    def late_result():
        return pltpu.make_async_remote_copy(
            src_ref=late_out, dst_ref=late_in, send_sem=misc_send, recv_sem=lr_recv,
            device_id={"row": lax.rem(row + n_row - 1, n_row)}, device_id_type=MESH,
        )

    def group(g):
        return (slice(0, lanes - 2), slice(1, 4), slice(4, lanes - 2), slice(lanes - 2, lanes))[g]

    def slot(p, g):
        if isinstance(p, int) and p >= panels:
            return 3 * panels + (g - 1 if p == late else 3)
        return 3 * p + (0, 0, 1, 2)[g]

    def pair_copy(p, m, g):
        place = (2 * m + 1 - core) * part
        return pltpu.make_async_remote_copy(
            src_ref=grad.at[p, group(g), pl.ds(pl.multiple_of(place, part), part)], dst_ref=rs_a.at[p, m, group(g)],
            send_sem=a_send, recv_sem=a_recv.at[slot(p, g)],
            device_id={"col": 2 * chip + 1 - core}, device_id_type=MESH,
        )

    def chip_copy(p, j, g):
        peer = lax.rem(chip + j, chips)
        return pltpu.make_async_remote_copy(
            src_ref=rs_a.at[p, peer, group(g)], dst_ref=rs_b.at[p, j, group(g)],
            send_sem=b_send, recv_sem=b_recv.at[slot(p, g)],
            device_id={"col": 2 * peer + core}, device_id_type=MESH,
        )

    def pair_all(p, g):
        return pltpu.make_async_remote_copy(
            src_ref=rs_a.at[p, :, group(g)], dst_ref=rs_a.at[p, :, group(g)],
            send_sem=a_send, recv_sem=a_recv.at[slot(p, g)],
            device_id={"col": 2 * chip + 1 - core}, device_id_type=MESH,
        )

    def chip_all(p, g):
        return pltpu.make_async_remote_copy(
            src_ref=rs_b.at[p, 1:, group(g)], dst_ref=rs_b.at[p, 1:, group(g)],
            send_sem=b_send, recv_sem=b_recv.at[slot(p, g)],
            device_id={"col": 2 * lax.rem(chip + 1, chips) + core}, device_id_type=MESH,
        )

    def y_all(p, first, sems, step):
        return pltpu.make_async_remote_copy(
            src_ref=y.at[p, first:], dst_ref=y.at[p, first:], send_sem=sems, recv_sem=recv_sem.at[0, 0],
            device_id={"row": lax.rem(row + step, n_row)}, device_id_type=MESH,
        )

    def own_all():
        return pltpu.make_async_remote_copy(
            src_ref=far_own, dst_ref=far_own, send_sem=misc_send, recv_sem=fo_recv.at[0],
            device_id={"row": lax.rem(row + 1, n_row)}, device_id_type=MESH,
        )

    def groups(p, act):
        if isinstance(p, int) and p >= panels:
            for g in (1, 2, 3) if p == late else (3,):
                act(g)
            return

        short = spared & (p >= last - 1)

        @pl.when(jnp.logical_not(short))
        def _():
            act(0)

        @pl.when(short)
        def _():
            act(1)
            act(2)

        @pl.when(row <= n_row - 1 - p)
        def _():
            act(3)

    def lower(p):
        inner = lax.broadcasted_iota(jnp.int32, (width, lane), 0)
        within = lax.broadcasted_iota(jnp.int32, (width, lane), 1)
        for k in range(2):
            at = lanes - 2 + k
            grad[p, at] = jnp.where(inner >= within + k * lane, grad[p, at], 0.0)

    def pair_group(p, g):
        for m in range(chips):
            pair_copy(p, m, g).start()

    def pair_start(p):
        if p < panels:
            @pl.when(row == n_row - 1 - p)
            def _():
                lower(p)

        groups(p, functools.partial(pair_group, p))

    def chip_start(p):
        def act(g):
            pair_all(p, g).wait_recv()
            for j in range(1, chips + 1):
                m = lax.rem(chip + j, chips)
                place = pl.multiple_of((2 * m + core) * part, part)
                rs_a[p, m, group(g)] += grad[p, group(g), pl.ds(place, part)]
                if j < chips:
                    chip_copy(p, j, g).start()

        groups(p, act)

    def total(p, b):
        value = rs_a[p, chip, b]
        for j in range(1, chips):
            value = value + rs_b[p, j, b]
        return value

    def finish(p):
        def act(g):
            chip_all(p, g).wait_recv()
            for b in range(lanes)[group(g)]:
                out_ref[p, :, b * lane : (b + 1) * lane] = total(p, b)

        out_ref[p, :, tail:] = jnp.zeros((part, width), F32)
        groups(p, act)

    def late_work():
        late_rows().wait_recv()
        yq = split(y[last, LATE])
        for b in range(blocks):
            value = product(yq, split(late_w[b * width : (b + 1) * width]), NT)
            grad[late, 2 * b] = -value[:, :lane]
            grad[late, 2 * b + 1] = -value[:, lane:]
        lower(late)
        pair_start(late)

    def corner_work():
        corner_rows().wait_recv()
        for k in range(2):
            value = None
            for c in range(count):
                term = product(split(y[last - 1 + k, c]), split(late_c[:, c * CHUNK : (c + 1) * CHUNK]), NT)
                value = term if value is None else value + term
            grad[corner, lanes - 2 + k] = -value
        pair_start(corner)

    def late_finish():
        def act(p, shift, g):
            chip_all(p, g).wait_recv()
            for b in range(lanes)[group(g)]:
                late_out[:, (b + shift) * lane : (b + shift + 1) * lane] = total(p, b)

        late_out[:, :lane] = jnp.zeros((part, lane), F32)
        groups(late, functools.partial(act, late, 0))
        groups(corner, functools.partial(act, corner, 2))
        late_result().start()

    def solve(p, c, own):
        y[p, c] = product((dth[p], dtl[p]), split(own), NN)

    def inverse(p):
        hi, lo = split(diag_ref[p].T)
        dth[p] = hi
        dtl[p] = lo

    def receive(p, c):
        root = n_row - 1 - p
        source = row == root
        if p == last:
            source = source | (row == helper)
        if p == last - 1:
            source = source | ((row == last_root) & ((c == RAW[0]) | (c == RAW[1])))
        if p == 1:
            source = source | (row == n_row - 1)
        for h in range(PIECES[p]):
            @pl.when(jnp.logical_not(source))
            def _():
                y_copy(p, c, h, down_sem, n_row - 1).wait_recv()

            @pl.when(jnp.logical_not(source) & (row > root) & (row < n_row - 1))
            def _():
                up(p, c, h).start()

            @pl.when((row > 0) & (row < root))
            def _():
                down(p, c, h).start()

    def send(p, c, way):
        for h in range(PIECES[p]):
            way(p, c, h).start()

    def tail_update(p, c):
        res_ref[tail:, columns(c)] -= product((pth[p, tail:], ptl[p, tail:]), split(y[p, c]), NN)

    def keep(p, c):
        @pl.when(row == n_row - 1 - p)
        def _():
            res_ref[tail:, columns(c)] = y[p, c]

    def grad_block(q, c, yq, b):
        at = slice(b * width, (b + 1) * width)
        value = product(yq, (wh[c, at], wl[c, at]), NT)
        grad[q, 2 * b] -= value[:, :lane]
        grad[q, 2 * b + 1] -= value[:, lane:]

    def grad_work(q, c):
        yq = split(y[q, c])
        for b in range(blocks):
            grad_block(q, c, yq, b)

    def grad_last(c):
        yq = split(y[last - 1, c])
        for b in range(blocks):
            grad_block(last - 1, c, yq, b)
            for g in range(1, 4):
                if group(g).stop == 2 * b + 2:
                    pair_group(last - 1, g)

    def res_work(q, c):
        yq = split(y[q, c])
        for b in range(blocks - 1):
            at = slice(b * width, (b + 1) * width)
            res_ref[at, columns(c)] -= product((pth[q, at], ptl[q, at]), yq, NN)

    def take_panels(n):
        panel_shares(n).wait_recv()
        for p in range(n):
            hi, lo = split(far_pan[p].T)
            fph[p] = hi
            fpl[p] = lo

    def far(q, c):
        far_rows(c, 1).wait_recv()
        own = far_own[c]
        for p in range(q):
            own = own - product((fph[p], fpl[p]), split(y[p, c]), NN)
        solve(q, c, own)

    def advance(p, c):
        root = n_row - 1 - p
        receive(p, c)

        @pl.when(row < root)
        def _():
            tail_update(p, c)

            @pl.when(row == root - 1)
            def _():
                solve(p + 1, c, res_ref[tail:, columns(c)])
                if p + 1 < last - 1:
                    send(p + 1, c, down)

                if p > 0:
                    send(p + 1, c, up)

        keep(p, c)

    def close(c):
        receive(last - 1, c)
        tail_update(last - 1, c)
        solve(last, c, res_ref[tail:, columns(c)])

        @pl.when(row > 0)
        def _():
            send(last, c, down)

        keep(last, c)
        for q in (last, last - 1):
            grad_work(q, c)
            res_work(q, c)

    barrier = pltpu.get_barrier_semaphore()
    for step in (1, n_row - 1):
        pl.semaphore_signal(barrier, inc=1, device_id={"row": lax.rem(row + step, n_row)}, device_id_type=MESH)
    for step in range(1, n_col):
        pl.semaphore_signal(barrier, inc=1, device_id={"col": lax.rem(col + step, n_col)}, device_id_type=MESH)

    diag_copy = pltpu.make_async_copy(diag_hbm, diag_ref, local_sem.at[0])
    tail_copy = pltpu.make_async_copy(cot_hbm.at[tail:], res_ref.at[tail:], local_sem.at[1])
    pan_copy = pltpu.make_async_copy(pan_hbm, pan_ref, local_sem.at[2])
    head_copy = pltpu.make_async_copy(cot_hbm.at[:tail], res_ref.at[:tail], local_sem.at[3])
    wht_copy = pltpu.make_async_copy(wht_hbm, wht_ref, local_sem.at[4])
    for copy in (diag_copy, tail_copy, pan_copy, wht_copy, head_copy):
        copy.start()
    pl.semaphore_wait(barrier, 2 + n_col - 1)

    @pl.when(row == helper)
    def _():
        panel_part(last - 1, n_row - 1).start()
        for c in RAW:
            far_rows(c, n_row - 1).start()

    @pl.when(row == n_row - 2)
    def _():
        panel_part(1, 1).start()

        @pl.loop(0, count)
        def _(c):
            far_rows(c, 1).start()

    @pl.when(row == last_root)
    def _():
        panel_part(last, 1).start()
        for c in range(LATE + 1):
            far_rows(c, 1).start()
        late_rows().start()

        @pl.loop(LATE + 1, count)
        def _(c):
            far_rows(c, 1).start()

        corner_rows().start()

    diag_copy.wait()
    inverse(0)
    tail_copy.wait()

    @pl.when(row == n_row - 1)
    def _():
        @pl.loop(0, count)
        def _(c):
            solve(0, c, res_ref[tail:, columns(c)])
            send(0, c, down)

    @pl.loop(1, panels)
    def _(p):
        inverse(p)

    pan_copy.wait()

    @pl.loop(0, panels)
    def _(p):
        for b in range(blocks):
            hi, lo = split(pan_ref[p, :, b * width : (b + 1) * width].T)
            pth[p, b * width : (b + 1) * width] = hi
            ptl[p, b * width : (b + 1) * width] = lo
        grad[p] = jnp.zeros(grad.shape[1:], F32)

    def share_panels(n, step):
        panel_part(n, step).wait_recv()
        for k in range(1, n_col):
            panel_share(n, k).start()

    @pl.when(row == helper)
    def _():
        share_panels(last, 1)

    @pl.when(row == last_root)
    def _():
        share_panels(last - 1, n_row - 1)

    @pl.when(row == n_row - 1)
    def _():
        share_panels(1, 1)

    wht_copy.wait()
    head_copy.wait()
    advance(0, 0)

    @pl.when(row == n_row - 1)
    def _():
        take_panels(1)

    @pl.when(row == helper)
    def _():
        take_panels(last)

    passing = (row > helper) & (row < n_row - 1)

    @pl.loop(0, count)
    def _(c):
        @pl.when(passing & (c == count - 1))
        def _():
            receive(last - 1, 0)

        hi, lo = split(wht_ref[:, columns(c)])
        wh[c] = hi
        wl[c] = lo
        grad_work(0, c)

        @pl.when(c == count - 1)
        def _():
            pair_start(0)

        res_work(0, c)

        @pl.when(c == count - 1)
        def _():
            chip_start(0)

        @pl.when(row == n_row - 1)
        def _():
            far(1, c)

        for p in range(1, last - 1):
            advance(p, c)

        @pl.when(row == helper)
        def _():
            @pl.when(c == count - 1)
            def _():
                @pl.loop(RAW[1] + 1, count)
                def _(k):
                    send(last - 1, k, down)

                send(last - 1, LATE, down)

            far(last, c)
            send(last, c, up)

            @pl.when(c == LATE + 1)
            def _():
                late_work()

        for q in range(1, last - 1):
            grad_work(q, c)

            @pl.when(c == count - 1)
            def _():
                pair_start(q)

            res_work(q, c)

        @pl.when(spared & (c >= 1) & (c <= 2))
        def _():
            @pl.when(c == 1)
            def _():
                take_panels(last - 1)

            r = (c - 1) * (RAW[1] - RAW[0]) + RAW[0]
            far(last - 1, r)
            close(r)

        @pl.when(c + 1 < count)
        def _():
            advance(0, c + 1)

        @pl.when(row == helper)
        def _():
            grad_work(last - 1, c)
            res_work(last - 1, c)

            @pl.when(c == LATE + 1)
            def _():
                chip_start(late)

    @pl.when(jnp.logical_not(passing))
    def _():
        for p in range(1, last - 1):
            chip_start(p)

    @pl.when(row == helper)
    def _():
        pair_start(last - 1)

    below = row < helper
    start = jnp.where(spared, len(RAW), 0)
    bulk = jnp.where(spared, count - 2, count - 1)

    @pl.loop(start, count)
    def _(t):
        c = jnp.where(below & (t > 0), jnp.where(t == count - 1, LATE, t + 1), t)

        @pl.when((row != helper) & ((t > 0) | jnp.logical_not(passing)))
        def _():
            receive(last - 1, c)

        @pl.when((row != helper) & jnp.logical_not(spared))
        def _():
            grad_work(last - 1, c)

            @pl.when(t == count - 1)
            def _():
                pair_start(last - 1)

        @pl.when(t > bulk)
        def _():
            grad_last(c)

        @pl.when(below)
        def _():
            tail_update(last - 1, c)

            @pl.when(spared)
            def _():
                solve(last, c, res_ref[tail:, columns(c)])

                @pl.when(row > 0)
                def _():
                    send(last, c, down)

        @pl.when(t > bulk)
        def _():
            chip_start(last - 1)

        keep(last - 1, c)

        @pl.when(row > helper)
        def _():
            res_work(last - 1, c)

            @pl.when((row == n_row - 1) & (t == count - 1))
            def _():
                chip_start(last - 1)

        receive(last, c)

        @pl.when(passing & (t == 0))
        def _():
            for p in range(1, last - 1):
                chip_start(p)

        @pl.when(row < last_root)
        def _():
            tail_update(last, c)

        keep(last, c)

        @pl.when((row > helper) & (row < n_row - 1) & (t == count - 1) | (row == helper) & (t == 0))
        def _():
            chip_start(last - 1)

        @pl.when(t <= bulk)
        def _():
            grad_work(last, c)

            @pl.when(t == bulk)
            def _():
                pair_start(last)

        @pl.when(spared & (t <= bulk))
        def _():
            grad_work(last - 1, c)

            @pl.when(t == bulk)
            def _():
                chip_start(last)

        @pl.when(row == helper)
        def _():
            @pl.when(t == 1)
            def _():
                corner_work()

            @pl.when(t == 2)
            def _():
                chip_start(corner)

        @pl.when(below)
        def _():
            res_work(last - 1, c)

        res_work(last, c)

    @pl.when(row < last_root)
    def _():
        chip_start(last - 1)

    @pl.when(jnp.logical_not(spared))
    def _():
        chip_start(last)

    for p in range(last - 1):
        finish(p)

    @pl.when(row == helper)
    def _():
        late_finish()

    @pl.loop(0, panels)
    def _(p):
        root = n_row - 1 - p
        groups(p, lambda g: pair_all(p, g).wait_send())

        @pl.when((row >= root) & (row < n_row - 1) & ((p < last) | (row > last_root)) & (p != 1))
        def _():
            y_all(p, 0, up_sem, 1).wait_send()

        @pl.when((row <= root) & (row > 0) & ((p != last - 1) | (row != helper)))
        def _():
            y_all(p, 0, down_sem, n_row - 1).wait_send()

    @pl.when(row == helper)
    def _():
        y_all(last - 1, len(RAW), down_sem, n_row - 1).wait_send()
        panel_part(last - 1, n_row - 1).wait_send()
        for c in RAW:
            far_rows(c, n_row - 1).wait_send()
        panel_shares(last).wait_send()
        for p in (late, corner):
            groups(p, lambda g: pair_all(p, g).wait_send())
            groups(p, lambda g: chip_all(p, g).wait_send())

    @pl.when(row == n_row - 2)
    def _():
        panel_part(1, 1).wait_send()
        own_all().wait_send()

    @pl.when(row == n_row - 1)
    def _():
        panel_shares(1).wait_send()

    @pl.when(spared)
    def _():
        panel_part(last, 1).wait_send()
        own_all().wait_send()
        panel_shares(last - 1).wait_send()
        late_rows().wait_send()
        corner_rows().wait_send()

    for p in range(last - 1):
        groups(p, lambda g: chip_all(p, g).wait_send())

    finish(last)
    finish(last - 1)

    @pl.when(spared)
    def _():
        late_result().wait_recv()
        out_ref[last - 1, :, :lane] = late_in[:, rows : rows + lane]
        out_ref[last, :, lane:] += late_in[:, lane:rows]
        out_ref[last, :, :lane] = late_in[:, rows + lane :]

    for p in (last - 1, last):
        groups(p, lambda g: chip_all(p, g).wait_send())

    @pl.when(row == helper)
    def _():
        late_result().wait_send()


def store_kernel(res_ref, grad_ref, res_hbm, grad_hbm, sems):
    step = res_ref.shape[0] // STORES
    copies = [pltpu.make_async_copy(grad_ref, grad_hbm, sems.at[STORES])]
    for k in range(STORES):
        at = slice(k * step, (k + 1) * step)
        copies.append(pltpu.make_async_copy(res_ref.at[at], res_hbm.at[at], sems.at[k]))
    for copy in copies:
        copy.start()
    for copy in copies:
        copy.wait()


def solution(mesh):
    n_row, n_col = mesh.shape["row"], mesh.shape["col"]

    def body(cotangent, whitened, panel_rows, diag_inverse):
        rows, rhs = cotangent.shape
        panels, width = diag_inverse.shape[:2]
        assert panels == len(PIECES) <= n_row and n_col % 2 == 0 and rhs // CHUNK > RAW[1] + 1
        count, blocks, part, chips = rhs // CHUNK, rows // width, width // n_col, n_col // 2
        anywhere = pl.BlockSpec(memory_space=pl.ANY)
        vmem = pl.BlockSpec(memory_space=pltpu.VMEM)
        hbm = pl.BlockSpec(memory_space=pltpu.HBM)
        dma = pltpu.SemaphoreType.DMA
        kept = pl.pallas_call(
            functools.partial(kernel, n_row, n_col),
            out_shape=(pltpu.VMEM((rows, rhs), F32), pltpu.VMEM((panels, part, rows), F32)),
            in_specs=[hbm] * 4,
            out_specs=(vmem, vmem),
            scratch_shapes=[
                pltpu.VMEM((rows, rhs), F32),
                pltpu.VMEM((panels, width, rows), F32),
                pltpu.VMEM((panels, width, width), F32),
                pltpu.VMEM((panels, count, width, CHUNK), F32),
                pltpu.VMEM((panels, rows, width), BF16),
                pltpu.VMEM((panels, rows, width), BF16),
                pltpu.VMEM((panels, width, width), BF16),
                pltpu.VMEM((panels, width, width), BF16),
                pltpu.VMEM((count, rows, CHUNK), BF16),
                pltpu.VMEM((count, rows, CHUNK), BF16),
                pltpu.VMEM((panels + 2, 2 * blocks, width, width // 2), F32),
                pltpu.VMEM((panels + 2, chips, 2 * blocks, part, width // 2), F32),
                pltpu.VMEM((panels + 2, chips, 2 * blocks, part, width // 2), F32),
                pltpu.VMEM((panels - 1, width, width), F32),
                pltpu.VMEM((count, width, CHUNK), F32),
                pltpu.VMEM((panels - 1, width, width), BF16),
                pltpu.VMEM((panels - 1, width, width), BF16),
                pltpu.VMEM((rows, CHUNK), F32),
                pltpu.VMEM((width // 2, rhs), F32),
                pltpu.VMEM((part, rows + width), F32),
                pltpu.VMEM((part, rows + width), F32),
                dma((5,)),
                dma((count, sum(PIECES))),
                dma,
                dma,
                dma,
                dma((3 * panels + 4,)),
                dma,
                dma((3 * panels + 4,)),
                dma,
                dma,
                dma((count,)),
                dma,
                dma,
                dma,
                dma,
            ],
            compiler_params=pltpu.CompilerParams(
                collective_id=0, has_side_effects=True, vmem_limit_bytes=117 * 512 * 1024
            ),
        )(cotangent, whitened, panel_rows, diag_inverse)
        return pl.pallas_call(
            store_kernel,
            out_shape=tuple(jax.ShapeDtypeStruct(k.shape, F32) for k in kept),
            in_specs=[anywhere] * 2,
            out_specs=(hbm, hbm),
            scratch_shapes=[dma((STORES + 1,))],
            compiler_params=pltpu.CompilerParams(vmem_limit_bytes=1024 * 1024),
        )(*kept)

    return jax.shard_map(
        body,
        mesh=mesh,
        in_specs=(P("row", "col"), P("row", "col"), P(None, None, "row"), P()),
        out_specs=(P("row", "col"), P(None, "col", "row")),
        check_vma=False,
    )
```

```python
import functools

import jax
import jax.numpy as jnp
from jax import lax
from jax.experimental import pallas as pl
from jax.experimental.pallas import tpu as pltpu
from jax.sharding import PartitionSpec as P

MESH = pl.DeviceIdType.MESH
CHUNK = 256
PIECES = (4, 4, 1, 2)
STORES = 4
RAW = (0, 2)
LATE = 1
F32 = jnp.float32
BF16 = jnp.bfloat16


def split(x):
    hi = x.astype(BF16)
    return hi, (x - hi.astype(F32)).astype(BF16)


def product(a, b, dims):
    dot = functools.partial(lax.dot_general, dimension_numbers=(dims, ((), ())), preferred_element_type=F32)
    return dot(a[0], b[0]) + (dot(a[0], b[1]) + dot(a[1], b[0]))


NN = ((1,), (0,))
NT = ((1,), (1,))


def kernel(
    n_row, n_col, cot_hbm, wht_hbm, pan_hbm, diag_hbm, res_ref, out_ref,
    wht_ref, pan_ref, diag_ref, y, pth, ptl, dth, dtl, wh, wl, grad, rs_a, rs_b,
    far_pan, far_own, fph, fpl, late_w, late_c, late_out, late_in,
    local_sem, recv_sem, down_sem, up_sem, a_send, a_recv, b_send, b_recv,
    misc_send, fp_recv, fo_recv, ag_recv, lw_recv, lc_recv, lr_recv,
):
    rows, rhs = res_ref.shape
    panels, width = diag_ref.shape[0], diag_ref.shape[1]
    count = rhs // CHUNK
    blocks = rows // width
    tail = rows - width
    part = width // n_col
    chips = n_col // 2
    offset = [sum(PIECES[:p]) for p in range(panels)]
    row, col = lax.axis_index("row"), lax.axis_index("col")
    core, chip = lax.rem(col, 2), col // 2
    last = panels - 1
    last_root = n_row - panels
    helper = last_root + 1
    spared = row == last_root
    lane = width // 2
    lanes = 2 * blocks
    late, corner = panels, panels + 1

    def columns(c):
        return pl.ds(pl.multiple_of(c * CHUNK, CHUNK), CHUNK)

    def y_copy(p, c, h, sems, step):
        piece = width // PIECES[p]
        block = y.at[p, c, h * piece : (h + 1) * piece]
        return pltpu.make_async_remote_copy(
            src_ref=block, dst_ref=block, send_sem=sems, recv_sem=recv_sem.at[c, offset[p] + h],
            device_id={"row": lax.rem(row + step, n_row)}, device_id_type=MESH,
        )

    def down(p, c, h):
        return y_copy(p, c, h, down_sem, n_row - 1)

    def up(p, c, h):
        return y_copy(p, c, h, up_sem, 1)

    own_part = pl.ds(pl.multiple_of(col * part, part), part)

    def panel_part(n, step):
        return pltpu.make_async_remote_copy(
            src_ref=pan_hbm.at[:n, own_part, tail:], dst_ref=far_pan.at[:n, own_part],
            send_sem=misc_send, recv_sem=fp_recv,
            device_id={"row": lax.rem(row + step, n_row)}, device_id_type=MESH,
        )

    def panel_share(n, step):
        return pltpu.make_async_remote_copy(
            src_ref=far_pan.at[:n, own_part], dst_ref=far_pan.at[:n, own_part],
            send_sem=misc_send, recv_sem=ag_recv,
            device_id={"col": lax.rem(col + step, n_col)}, device_id_type=MESH,
        )

    def panel_shares(n):
        others = far_pan.at[:n, : (n_col - 1) * part]
        return pltpu.make_async_remote_copy(
            src_ref=others, dst_ref=others, send_sem=misc_send, recv_sem=ag_recv,
            device_id={"col": lax.rem(col + 1, n_col)}, device_id_type=MESH,
        )

    def far_rows(c, step):
        return pltpu.make_async_remote_copy(
            src_ref=cot_hbm.at[tail:, columns(c)], dst_ref=far_own.at[c], send_sem=misc_send, recv_sem=fo_recv.at[c],
            device_id={"row": lax.rem(row + step, n_row)}, device_id_type=MESH,
        )

    def late_rows():
        return pltpu.make_async_remote_copy(
            src_ref=wht_hbm.at[:, columns(LATE)], dst_ref=late_w, send_sem=misc_send, recv_sem=lw_recv,
            device_id={"row": lax.rem(row + 1, n_row)}, device_id_type=MESH,
        )

    def corner_rows():
        return pltpu.make_async_remote_copy(
            src_ref=wht_hbm.at[:lane], dst_ref=late_c, send_sem=misc_send, recv_sem=lc_recv,
            device_id={"row": lax.rem(row + 1, n_row)}, device_id_type=MESH,
        )

    def late_result():
        return pltpu.make_async_remote_copy(
            src_ref=late_out, dst_ref=late_in, send_sem=misc_send, recv_sem=lr_recv,
            device_id={"row": lax.rem(row + n_row - 1, n_row)}, device_id_type=MESH,
        )

    def group(g):
        return (slice(0, lanes - 2), slice(1, 4), slice(4, lanes - 2), slice(lanes - 2, lanes))[g]

    def slot(p, g):
        if isinstance(p, int) and p >= panels:
            return 3 * panels + (g - 1 if p == late else 3)
        return 3 * p + (0, 0, 1, 2)[g]

    def pair_copy(p, m, g):
        place = (2 * m + 1 - core) * part
        return pltpu.make_async_remote_copy(
            src_ref=grad.at[p, group(g), pl.ds(pl.multiple_of(place, part), part)], dst_ref=rs_a.at[p, m, group(g)],
            send_sem=a_send, recv_sem=a_recv.at[slot(p, g)],
            device_id={"col": 2 * chip + 1 - core}, device_id_type=MESH,
        )

    def chip_copy(p, j, g):
        peer = lax.rem(chip + j, chips)
        return pltpu.make_async_remote_copy(
            src_ref=rs_a.at[p, peer, group(g)], dst_ref=rs_b.at[p, j, group(g)],
            send_sem=b_send, recv_sem=b_recv.at[slot(p, g)],
            device_id={"col": 2 * peer + core}, device_id_type=MESH,
        )

    def pair_all(p, g):
        return pltpu.make_async_remote_copy(
            src_ref=rs_a.at[p, :, group(g)], dst_ref=rs_a.at[p, :, group(g)],
            send_sem=a_send, recv_sem=a_recv.at[slot(p, g)],
            device_id={"col": 2 * chip + 1 - core}, device_id_type=MESH,
        )

    def chip_all(p, g):
        return pltpu.make_async_remote_copy(
            src_ref=rs_b.at[p, 1:, group(g)], dst_ref=rs_b.at[p, 1:, group(g)],
            send_sem=b_send, recv_sem=b_recv.at[slot(p, g)],
            device_id={"col": 2 * lax.rem(chip + 1, chips) + core}, device_id_type=MESH,
        )

    def y_all(p, first, sems, step):
        return pltpu.make_async_remote_copy(
            src_ref=y.at[p, first:], dst_ref=y.at[p, first:], send_sem=sems, recv_sem=recv_sem.at[0, 0],
            device_id={"row": lax.rem(row + step, n_row)}, device_id_type=MESH,
        )

    def own_all():
        return pltpu.make_async_remote_copy(
            src_ref=far_own, dst_ref=far_own, send_sem=misc_send, recv_sem=fo_recv.at[0],
            device_id={"row": lax.rem(row + 1, n_row)}, device_id_type=MESH,
        )

    def groups(p, act):
        if isinstance(p, int) and p >= panels:
            for g in (1, 2, 3) if p == late else (3,):
                act(g)
            return

        short = spared & (p >= last - 1)

        @pl.when(jnp.logical_not(short))
        def _():
            act(0)

        @pl.when(short)
        def _():
            act(1)
            act(2)

        @pl.when(row <= n_row - 1 - p)
        def _():
            act(3)

    def lower(p):
        inner = lax.broadcasted_iota(jnp.int32, (width, lane), 0)
        within = lax.broadcasted_iota(jnp.int32, (width, lane), 1)
        for k in range(2):
            at = lanes - 2 + k
            grad[p, at] = jnp.where(inner >= within + k * lane, grad[p, at], 0.0)

    def pair_group(p, g):
        for m in range(chips):
            pair_copy(p, m, g).start()

    def pair_start(p):
        if p < panels:
            @pl.when(row == n_row - 1 - p)
            def _():
                lower(p)

        groups(p, functools.partial(pair_group, p))

    def chip_start(p):
        def act(g):
            pair_all(p, g).wait_recv()
            for j in range(1, chips + 1):
                m = lax.rem(chip + j, chips)
                place = pl.multiple_of((2 * m + core) * part, part)
                rs_a[p, m, group(g)] += grad[p, group(g), pl.ds(place, part)]
                if j < chips:
                    chip_copy(p, j, g).start()

        groups(p, act)

    def total(p, b):
        value = rs_a[p, chip, b]
        for j in range(1, chips):
            value = value + rs_b[p, j, b]
        return value

    def finish(p):
        def act(g):
            chip_all(p, g).wait_recv()
            for b in range(lanes)[group(g)]:
                out_ref[p, :, b * lane : (b + 1) * lane] = total(p, b)

        out_ref[p, :, tail:] = jnp.zeros((part, width), F32)
        groups(p, act)

    def late_work():
        late_rows().wait_recv()
        yq = split(y[last, LATE])
        for b in range(blocks):
            value = product(yq, split(late_w[b * width : (b + 1) * width]), NT)
            grad[late, 2 * b] = -value[:, :lane]
            grad[late, 2 * b + 1] = -value[:, lane:]
        lower(late)
        pair_start(late)

    def corner_work():
        corner_rows().wait_recv()
        for k in range(2):
            value = None
            for c in range(count):
                term = product(split(y[last - 1 + k, c]), split(late_c[:, c * CHUNK : (c + 1) * CHUNK]), NT)
                value = term if value is None else value + term
            grad[corner, lanes - 2 + k] = -value
        pair_start(corner)

    def late_finish():
        def act(p, shift, g):
            chip_all(p, g).wait_recv()
            for b in range(lanes)[group(g)]:
                late_out[:, (b + shift) * lane : (b + shift + 1) * lane] = total(p, b)

        late_out[:, :lane] = jnp.zeros((part, lane), F32)
        groups(late, functools.partial(act, late, 0))
        groups(corner, functools.partial(act, corner, 2))
        late_result().start()

    def solve(p, c, own):
        y[p, c] = product((dth[p], dtl[p]), split(own), NN)

    def inverse(p):
        hi, lo = split(diag_ref[p].T)
        dth[p] = hi
        dtl[p] = lo

    def receive(p, c):
        root = n_row - 1 - p
        source = row == root
        if p == last:
            source = source | (row == helper)
        if p == last - 1:
            source = source | ((row == last_root) & ((c == RAW[0]) | (c == RAW[1])))
        if p == 1:
            source = source | (row == n_row - 1)
        for h in range(PIECES[p]):
            @pl.when(jnp.logical_not(source))
            def _():
                y_copy(p, c, h, down_sem, n_row - 1).wait_recv()

            @pl.when(jnp.logical_not(source) & (row > root) & (row < n_row - 1))
            def _():
                up(p, c, h).start()

            @pl.when((row > 0) & (row < root))
            def _():
                down(p, c, h).start()

    def send(p, c, way):
        for h in range(PIECES[p]):
            way(p, c, h).start()

    def tail_update(p, c):
        res_ref[tail:, columns(c)] -= product((pth[p, tail:], ptl[p, tail:]), split(y[p, c]), NN)

    def keep(p, c):
        @pl.when(row == n_row - 1 - p)
        def _():
            res_ref[tail:, columns(c)] = y[p, c]

    def grad_block(q, c, yq, b):
        at = slice(b * width, (b + 1) * width)
        value = product(yq, (wh[c, at], wl[c, at]), NT)
        grad[q, 2 * b] -= value[:, :lane]
        grad[q, 2 * b + 1] -= value[:, lane:]

    def grad_work(q, c):
        yq = split(y[q, c])
        for b in range(blocks):
            grad_block(q, c, yq, b)

    def grad_last(q, c):
        yq = split(y[q, c])
        for b in range(blocks):
            grad_block(q, c, yq, b)
            if q == last and b == blocks - 1:
                lower(q)
            for g in range(1, 4):
                if group(g).stop == 2 * b + 2:
                    pair_group(q, g)

    def res_work(q, c):
        yq = split(y[q, c])
        for b in range(blocks - 1):
            at = slice(b * width, (b + 1) * width)
            res_ref[at, columns(c)] -= product((pth[q, at], ptl[q, at]), yq, NN)

    def take_panels(n):
        panel_shares(n).wait_recv()
        for p in range(n):
            hi, lo = split(far_pan[p].T)
            fph[p] = hi
            fpl[p] = lo

    def far(q, c):
        far_rows(c, 1).wait_recv()
        own = far_own[c]
        for p in range(q):
            own = own - product((fph[p], fpl[p]), split(y[p, c]), NN)
        solve(q, c, own)

    def advance(p, c):
        root = n_row - 1 - p
        receive(p, c)

        @pl.when(row < root)
        def _():
            tail_update(p, c)

            @pl.when(row == root - 1)
            def _():
                solve(p + 1, c, res_ref[tail:, columns(c)])
                if p + 1 < last - 1:
                    send(p + 1, c, down)

                if p > 0:
                    send(p + 1, c, up)

        keep(p, c)

    def close(c):
        receive(last - 1, c)
        tail_update(last - 1, c)
        solve(last, c, res_ref[tail:, columns(c)])

        @pl.when(row > 0)
        def _():
            send(last, c, down)

        keep(last, c)
        for q in (last, last - 1):
            grad_work(q, c)
            res_work(q, c)

    barrier = pltpu.get_barrier_semaphore()
    for step in (1, n_row - 1):
        pl.semaphore_signal(barrier, inc=1, device_id={"row": lax.rem(row + step, n_row)}, device_id_type=MESH)
    for step in range(1, n_col):
        pl.semaphore_signal(barrier, inc=1, device_id={"col": lax.rem(col + step, n_col)}, device_id_type=MESH)

    diag_copy = pltpu.make_async_copy(diag_hbm, diag_ref, local_sem.at[0])
    tail_copy = pltpu.make_async_copy(cot_hbm.at[tail:], res_ref.at[tail:], local_sem.at[1])
    pan_copy = pltpu.make_async_copy(pan_hbm, pan_ref, local_sem.at[2])
    head_copy = pltpu.make_async_copy(cot_hbm.at[:tail], res_ref.at[:tail], local_sem.at[3])
    wht_copy = pltpu.make_async_copy(wht_hbm, wht_ref, local_sem.at[4])
    for copy in (diag_copy, tail_copy, pan_copy, wht_copy, head_copy):
        copy.start()
    pl.semaphore_wait(barrier, 2 + n_col - 1)

    @pl.when(row == helper)
    def _():
        panel_part(last - 1, n_row - 1).start()
        for c in RAW:
            far_rows(c, n_row - 1).start()

    @pl.when(row == n_row - 2)
    def _():
        panel_part(1, 1).start()

        @pl.loop(0, count)
        def _(c):
            far_rows(c, 1).start()

    @pl.when(row == last_root)
    def _():
        panel_part(last, 1).start()
        for c in range(LATE + 1):
            far_rows(c, 1).start()
        late_rows().start()

        @pl.loop(LATE + 1, count)
        def _(c):
            far_rows(c, 1).start()

        corner_rows().start()

    diag_copy.wait()
    inverse(0)
    tail_copy.wait()

    @pl.when(row == n_row - 1)
    def _():
        @pl.loop(0, count)
        def _(c):
            solve(0, c, res_ref[tail:, columns(c)])
            send(0, c, down)

    @pl.loop(1, panels)
    def _(p):
        inverse(p)

    pan_copy.wait()

    @pl.loop(0, panels)
    def _(p):
        for b in range(blocks):
            hi, lo = split(pan_ref[p, :, b * width : (b + 1) * width].T)
            pth[p, b * width : (b + 1) * width] = hi
            ptl[p, b * width : (b + 1) * width] = lo
        grad[p] = jnp.zeros(grad.shape[1:], F32)

    def share_panels(n, step):
        panel_part(n, step).wait_recv()
        for k in range(1, n_col):
            panel_share(n, k).start()

    @pl.when(row == helper)
    def _():
        share_panels(last, 1)

    @pl.when(row == last_root)
    def _():
        share_panels(last - 1, n_row - 1)

    @pl.when(row == n_row - 1)
    def _():
        share_panels(1, 1)

    wht_copy.wait()
    head_copy.wait()
    advance(0, 0)

    @pl.when(row == n_row - 1)
    def _():
        take_panels(1)

    @pl.when(row == helper)
    def _():
        take_panels(last)

    passing = (row > helper) & (row < n_row - 1)

    @pl.loop(0, count)
    def _(c):
        @pl.when(passing & (c == count - 1))
        def _():
            receive(last - 1, 0)

        hi, lo = split(wht_ref[:, columns(c)])
        wh[c] = hi
        wl[c] = lo
        grad_work(0, c)

        @pl.when(c == count - 1)
        def _():
            pair_start(0)

        res_work(0, c)

        @pl.when(c == count - 1)
        def _():
            chip_start(0)

        @pl.when(row == n_row - 1)
        def _():
            far(1, c)

        for p in range(1, last - 1):
            advance(p, c)

        @pl.when(row == helper)
        def _():
            @pl.when(c == count - 1)
            def _():
                @pl.loop(RAW[1] + 1, count)
                def _(k):
                    send(last - 1, k, down)

                send(last - 1, LATE, down)

            far(last, c)
            send(last, c, up)

            @pl.when(c == LATE + 1)
            def _():
                late_work()

        for q in range(1, last - 1):
            grad_work(q, c)

            @pl.when(c == count - 1)
            def _():
                pair_start(q)

            res_work(q, c)

        @pl.when(spared & (c >= 1) & (c <= 2))
        def _():
            @pl.when(c == 1)
            def _():
                take_panels(last - 1)

            r = (c - 1) * (RAW[1] - RAW[0]) + RAW[0]
            far(last - 1, r)
            close(r)

        @pl.when(c + 1 < count)
        def _():
            advance(0, c + 1)

        @pl.when(row == helper)
        def _():
            grad_work(last - 1, c)
            res_work(last - 1, c)

            @pl.when(c == LATE + 1)
            def _():
                chip_start(late)

    @pl.when(jnp.logical_not(passing))
    def _():
        for p in range(1, last - 1):
            chip_start(p)

    @pl.when(row == helper)
    def _():
        pair_start(last - 1)

    below = row < helper
    start = jnp.where(spared, len(RAW), 0)
    bulk = jnp.where(spared, count - 2, count - 1)

    @pl.loop(start, count)
    def _(t):
        c = jnp.where(below & (t > 0), jnp.where(t == count - 1, LATE, t + 1), t)

        @pl.when((row != helper) & ((t > 0) | jnp.logical_not(passing)))
        def _():
            receive(last - 1, c)

        @pl.when((row != helper) & jnp.logical_not(spared))
        def _():
            grad_work(last - 1, c)

            @pl.when(t == count - 1)
            def _():
                pair_start(last - 1)

        @pl.when(t > bulk)
        def _():
            grad_last(last - 1, c)

        @pl.when(below)
        def _():
            tail_update(last - 1, c)

            @pl.when(spared)
            def _():
                solve(last, c, res_ref[tail:, columns(c)])

                @pl.when(row > 0)
                def _():
                    send(last, c, down)

        @pl.when(t > bulk)
        def _():
            chip_start(last - 1)

        keep(last - 1, c)

        @pl.when(row > helper)
        def _():
            res_work(last - 1, c)

            @pl.when((row == n_row - 1) & (t == count - 1))
            def _():
                chip_start(last - 1)

        receive(last, c)

        @pl.when(passing & (t == 0))
        def _():
            for p in range(1, last - 1):
                chip_start(p)

        @pl.when(row < last_root)
        def _():
            tail_update(last, c)

        keep(last, c)

        @pl.when((row > helper) & (row < n_row - 1) & (t == count - 1) | (row == helper) & (t == 0))
        def _():
            chip_start(last - 1)

        @pl.when((t < bulk) | jnp.logical_not(spared))
        def _():
            grad_work(last, c)

            @pl.when(t == bulk)
            def _():
                pair_start(last)

        @pl.when(spared & (t == bulk))
        def _():
            grad_last(last, c)
            chip_start(last)

        @pl.when(spared & (t <= bulk))
        def _():
            grad_work(last - 1, c)

        @pl.when(row == helper)
        def _():
            @pl.when(t == 1)
            def _():
                corner_work()

            @pl.when(t == 2)
            def _():
                chip_start(corner)

        @pl.when(below)
        def _():
            res_work(last - 1, c)

        res_work(last, c)

    @pl.when(row < last_root)
    def _():
        chip_start(last - 1)

    @pl.when(jnp.logical_not(spared))
    def _():
        chip_start(last)

    for p in range(last - 1):
        finish(p)

    @pl.when(row == helper)
    def _():
        late_finish()

    @pl.loop(0, panels)
    def _(p):
        root = n_row - 1 - p
        groups(p, lambda g: pair_all(p, g).wait_send())

        @pl.when((row >= root) & (row < n_row - 1) & ((p < last) | (row > last_root)) & (p != 1))
        def _():
            y_all(p, 0, up_sem, 1).wait_send()

        @pl.when((row <= root) & (row > 0) & ((p != last - 1) | (row != helper)))
        def _():
            y_all(p, 0, down_sem, n_row - 1).wait_send()

    @pl.when(row == helper)
    def _():
        y_all(last - 1, len(RAW), down_sem, n_row - 1).wait_send()
        panel_part(last - 1, n_row - 1).wait_send()
        for c in RAW:
            far_rows(c, n_row - 1).wait_send()
        panel_shares(last).wait_send()
        for p in (late, corner):
            groups(p, lambda g: pair_all(p, g).wait_send())
            groups(p, lambda g: chip_all(p, g).wait_send())

    @pl.when(row == n_row - 2)
    def _():
        panel_part(1, 1).wait_send()
        own_all().wait_send()

    @pl.when(row == n_row - 1)
    def _():
        panel_shares(1).wait_send()

    @pl.when(spared)
    def _():
        panel_part(last, 1).wait_send()
        own_all().wait_send()
        panel_shares(last - 1).wait_send()
        late_rows().wait_send()
        corner_rows().wait_send()

    for p in range(last - 1):
        groups(p, lambda g: chip_all(p, g).wait_send())

    finish(last)
    finish(last - 1)

    @pl.when(spared)
    def _():
        late_result().wait_recv()
        out_ref[last - 1, :, :lane] = late_in[:, rows : rows + lane]
        out_ref[last, :, lane:] += late_in[:, lane:rows]
        out_ref[last, :, :lane] = late_in[:, rows + lane :]

    for p in (last - 1, last):
        groups(p, lambda g: chip_all(p, g).wait_send())

    @pl.when(row == helper)
    def _():
        late_result().wait_send()


def store_kernel(res_ref, grad_ref, res_hbm, grad_hbm, sems):
    step = res_ref.shape[0] // STORES
    copies = [pltpu.make_async_copy(grad_ref, grad_hbm, sems.at[STORES])]
    for k in range(STORES):
        at = slice(k * step, (k + 1) * step)
        copies.append(pltpu.make_async_copy(res_ref.at[at], res_hbm.at[at], sems.at[k]))
    for copy in copies:
        copy.start()
    for copy in copies:
        copy.wait()


def solution(mesh):
    n_row, n_col = mesh.shape["row"], mesh.shape["col"]

    def body(cotangent, whitened, panel_rows, diag_inverse):
        rows, rhs = cotangent.shape
        panels, width = diag_inverse.shape[:2]
        assert panels == len(PIECES) <= n_row and n_col % 2 == 0 and rhs // CHUNK > RAW[1] + 1
        count, blocks, part, chips = rhs // CHUNK, rows // width, width // n_col, n_col // 2
        anywhere = pl.BlockSpec(memory_space=pl.ANY)
        vmem = pl.BlockSpec(memory_space=pltpu.VMEM)
        hbm = pl.BlockSpec(memory_space=pltpu.HBM)
        dma = pltpu.SemaphoreType.DMA
        kept = pl.pallas_call(
            functools.partial(kernel, n_row, n_col),
            out_shape=(pltpu.VMEM((rows, rhs), F32), pltpu.VMEM((panels, part, rows), F32)),
            in_specs=[hbm] * 4,
            out_specs=(vmem, vmem),
            scratch_shapes=[
                pltpu.VMEM((rows, rhs), F32),
                pltpu.VMEM((panels, width, rows), F32),
                pltpu.VMEM((panels, width, width), F32),
                pltpu.VMEM((panels, count, width, CHUNK), F32),
                pltpu.VMEM((panels, rows, width), BF16),
                pltpu.VMEM((panels, rows, width), BF16),
                pltpu.VMEM((panels, width, width), BF16),
                pltpu.VMEM((panels, width, width), BF16),
                pltpu.VMEM((count, rows, CHUNK), BF16),
                pltpu.VMEM((count, rows, CHUNK), BF16),
                pltpu.VMEM((panels + 2, 2 * blocks, width, width // 2), F32),
                pltpu.VMEM((panels + 2, chips, 2 * blocks, part, width // 2), F32),
                pltpu.VMEM((panels + 2, chips, 2 * blocks, part, width // 2), F32),
                pltpu.VMEM((panels - 1, width, width), F32),
                pltpu.VMEM((count, width, CHUNK), F32),
                pltpu.VMEM((panels - 1, width, width), BF16),
                pltpu.VMEM((panels - 1, width, width), BF16),
                pltpu.VMEM((rows, CHUNK), F32),
                pltpu.VMEM((width // 2, rhs), F32),
                pltpu.VMEM((part, rows + width), F32),
                pltpu.VMEM((part, rows + width), F32),
                dma((5,)),
                dma((count, sum(PIECES))),
                dma,
                dma,
                dma,
                dma((3 * panels + 4,)),
                dma,
                dma((3 * panels + 4,)),
                dma,
                dma,
                dma((count,)),
                dma,
                dma,
                dma,
                dma,
            ],
            compiler_params=pltpu.CompilerParams(
                collective_id=0, has_side_effects=True, vmem_limit_bytes=117 * 512 * 1024
            ),
        )(cotangent, whitened, panel_rows, diag_inverse)
        return pl.pallas_call(
            store_kernel,
            out_shape=tuple(jax.ShapeDtypeStruct(k.shape, F32) for k in kept),
            in_specs=[anywhere] * 2,
            out_specs=(hbm, hbm),
            scratch_shapes=[dma((STORES + 1,))],
            compiler_params=pltpu.CompilerParams(vmem_limit_bytes=1024 * 1024),
        )(*kept)

    return jax.shard_map(
        body,
        mesh=mesh,
        in_specs=(P("row", "col"), P("row", "col"), P(None, None, "row"), P()),
        out_specs=(P("row", "col"), P(None, "col", "row")),
        check_vma=False,
    )
```

```python
import functools

import jax
import jax.numpy as jnp
from jax import lax
from jax.experimental import pallas as pl
from jax.experimental.pallas import tpu as pltpu
from jax.sharding import PartitionSpec as P

MESH = pl.DeviceIdType.MESH
CHUNK = 256
PIECES = (4, 4, 1, 2)
STORES = 1
RAW = (0, 2)
LATE = 1
F32 = jnp.float32
BF16 = jnp.bfloat16


def split(x):
    hi = x.astype(BF16)
    return hi, (x - hi.astype(F32)).astype(BF16)


def product(a, b, dims):
    dot = functools.partial(lax.dot_general, dimension_numbers=(dims, ((), ())), preferred_element_type=F32)
    return dot(a[0], b[0]) + (dot(a[0], b[1]) + dot(a[1], b[0]))


NN = ((1,), (0,))
NT = ((1,), (1,))


def kernel(
    n_row, n_col, cot_hbm, wht_hbm, pan_hbm, diag_hbm, res_ref, out_ref,
    wht_ref, pan_ref, diag_ref, y, pth, ptl, dth, dtl, wh, wl, grad, rs_a, rs_b,
    far_pan, far_own, fph, fpl, late_w, late_c, late_out, late_in,
    local_sem, recv_sem, down_sem, up_sem, a_send, a_recv, b_send, b_recv,
    misc_send, fp_recv, fo_recv, ag_recv, lw_recv, lc_recv, lr_recv,
):
    rows, rhs = res_ref.shape
    panels, width = diag_ref.shape[0], diag_ref.shape[1]
    count = rhs // CHUNK
    blocks = rows // width
    tail = rows - width
    part = width // n_col
    chips = n_col // 2
    offset = [sum(PIECES[:p]) for p in range(panels)]
    row, col = lax.axis_index("row"), lax.axis_index("col")
    core, chip = lax.rem(col, 2), col // 2
    last = panels - 1
    last_root = n_row - panels
    helper = last_root + 1
    spared = row == last_root
    lane = width // 2
    lanes = 2 * blocks
    late, corner = panels, panels + 1

    def columns(c):
        return pl.ds(pl.multiple_of(c * CHUNK, CHUNK), CHUNK)

    def y_copy(p, c, h, sems, step):
        piece = width // PIECES[p]
        block = y.at[p, c, h * piece : (h + 1) * piece]
        return pltpu.make_async_remote_copy(
            src_ref=block, dst_ref=block, send_sem=sems, recv_sem=recv_sem.at[c, offset[p] + h],
            device_id={"row": lax.rem(row + step, n_row)}, device_id_type=MESH,
        )

    def down(p, c, h):
        return y_copy(p, c, h, down_sem, n_row - 1)

    def up(p, c, h):
        return y_copy(p, c, h, up_sem, 1)

    own_part = pl.ds(pl.multiple_of(col * part, part), part)

    def panel_part(n, step):
        return pltpu.make_async_remote_copy(
            src_ref=pan_hbm.at[:n, own_part, tail:], dst_ref=far_pan.at[:n, own_part],
            send_sem=misc_send, recv_sem=fp_recv,
            device_id={"row": lax.rem(row + step, n_row)}, device_id_type=MESH,
        )

    def panel_share(n, step):
        return pltpu.make_async_remote_copy(
            src_ref=far_pan.at[:n, own_part], dst_ref=far_pan.at[:n, own_part],
            send_sem=misc_send, recv_sem=ag_recv,
            device_id={"col": lax.rem(col + step, n_col)}, device_id_type=MESH,
        )

    def panel_shares(n):
        others = far_pan.at[:n, : (n_col - 1) * part]
        return pltpu.make_async_remote_copy(
            src_ref=others, dst_ref=others, send_sem=misc_send, recv_sem=ag_recv,
            device_id={"col": lax.rem(col + 1, n_col)}, device_id_type=MESH,
        )

    def far_rows(c, step):
        return pltpu.make_async_remote_copy(
            src_ref=cot_hbm.at[tail:, columns(c)], dst_ref=far_own.at[c], send_sem=misc_send, recv_sem=fo_recv.at[c],
            device_id={"row": lax.rem(row + step, n_row)}, device_id_type=MESH,
        )

    def late_rows():
        return pltpu.make_async_remote_copy(
            src_ref=wht_hbm.at[:, columns(LATE)], dst_ref=late_w, send_sem=misc_send, recv_sem=lw_recv,
            device_id={"row": lax.rem(row + 1, n_row)}, device_id_type=MESH,
        )

    def corner_rows():
        return pltpu.make_async_remote_copy(
            src_ref=wht_hbm.at[:lane], dst_ref=late_c, send_sem=misc_send, recv_sem=lc_recv,
            device_id={"row": lax.rem(row + 1, n_row)}, device_id_type=MESH,
        )

    def late_result():
        return pltpu.make_async_remote_copy(
            src_ref=late_out, dst_ref=late_in, send_sem=misc_send, recv_sem=lr_recv,
            device_id={"row": lax.rem(row + n_row - 1, n_row)}, device_id_type=MESH,
        )

    def group(g):
        return (slice(0, lanes - 2), slice(1, 4), slice(4, lanes - 2), slice(lanes - 2, lanes))[g]

    def slot(p, g):
        if isinstance(p, int) and p >= panels:
            return 3 * panels + (g - 1 if p == late else 3)
        return 3 * p + (0, 0, 1, 2)[g]

    def pair_copy(p, m, g):
        place = (2 * m + 1 - core) * part
        return pltpu.make_async_remote_copy(
            src_ref=grad.at[p, group(g), pl.ds(pl.multiple_of(place, part), part)], dst_ref=rs_a.at[p, m, group(g)],
            send_sem=a_send, recv_sem=a_recv.at[slot(p, g)],
            device_id={"col": 2 * chip + 1 - core}, device_id_type=MESH,
        )

    def chip_copy(p, j, g):
        peer = lax.rem(chip + j, chips)
        return pltpu.make_async_remote_copy(
            src_ref=rs_a.at[p, peer, group(g)], dst_ref=rs_b.at[p, j, group(g)],
            send_sem=b_send, recv_sem=b_recv.at[slot(p, g)],
            device_id={"col": 2 * peer + core}, device_id_type=MESH,
        )

    def pair_all(p, g):
        return pltpu.make_async_remote_copy(
            src_ref=rs_a.at[p, :, group(g)], dst_ref=rs_a.at[p, :, group(g)],
            send_sem=a_send, recv_sem=a_recv.at[slot(p, g)],
            device_id={"col": 2 * chip + 1 - core}, device_id_type=MESH,
        )

    def chip_all(p, g):
        return pltpu.make_async_remote_copy(
            src_ref=rs_b.at[p, 1:, group(g)], dst_ref=rs_b.at[p, 1:, group(g)],
            send_sem=b_send, recv_sem=b_recv.at[slot(p, g)],
            device_id={"col": 2 * lax.rem(chip + 1, chips) + core}, device_id_type=MESH,
        )

    def y_all(p, first, sems, step):
        return pltpu.make_async_remote_copy(
            src_ref=y.at[p, first:], dst_ref=y.at[p, first:], send_sem=sems, recv_sem=recv_sem.at[0, 0],
            device_id={"row": lax.rem(row + step, n_row)}, device_id_type=MESH,
        )

    def own_all():
        return pltpu.make_async_remote_copy(
            src_ref=far_own, dst_ref=far_own, send_sem=misc_send, recv_sem=fo_recv.at[0],
            device_id={"row": lax.rem(row + 1, n_row)}, device_id_type=MESH,
        )

    def groups(p, act):
        if isinstance(p, int) and p >= panels:
            for g in (1, 2, 3) if p == late else (3,):
                act(g)
            return

        short = spared & (p >= last - 1)

        @pl.when(jnp.logical_not(short))
        def _():
            act(0)

        @pl.when(short)
        def _():
            act(1)
            act(2)

        @pl.when(row <= n_row - 1 - p)
        def _():
            act(3)

    def lower(p):
        inner = lax.broadcasted_iota(jnp.int32, (width, lane), 0)
        within = lax.broadcasted_iota(jnp.int32, (width, lane), 1)
        for k in range(2):
            at = lanes - 2 + k
            grad[p, at] = jnp.where(inner >= within + k * lane, grad[p, at], 0.0)

    def pair_group(p, g):
        for m in range(chips):
            pair_copy(p, m, g).start()

    def pair_start(p):
        if p < panels:
            @pl.when(row == n_row - 1 - p)
            def _():
                lower(p)

        groups(p, functools.partial(pair_group, p))

    def chip_start(p):
        def act(g):
            pair_all(p, g).wait_recv()
            for j in range(1, chips + 1):
                m = lax.rem(chip + j, chips)
                place = pl.multiple_of((2 * m + core) * part, part)
                rs_a[p, m, group(g)] += grad[p, group(g), pl.ds(place, part)]
                if j < chips:
                    chip_copy(p, j, g).start()

        groups(p, act)

    def total(p, b):
        value = rs_a[p, chip, b]
        for j in range(1, chips):
            value = value + rs_b[p, j, b]
        return value

    def finish(p):
        def act(g):
            chip_all(p, g).wait_recv()
            for b in range(lanes)[group(g)]:
                out_ref[p, :, b * lane : (b + 1) * lane] = total(p, b)

        out_ref[p, :, tail:] = jnp.zeros((part, width), F32)
        groups(p, act)

    def late_work():
        late_rows().wait_recv()
        yq = split(y[last, LATE])
        for b in range(blocks):
            value = product(yq, split(late_w[b * width : (b + 1) * width]), NT)
            grad[late, 2 * b] = -value[:, :lane]
            grad[late, 2 * b + 1] = -value[:, lane:]
        lower(late)
        pair_start(late)

    def corner_work():
        corner_rows().wait_recv()
        for k in range(2):
            value = None
            for c in range(count):
                term = product(split(y[last - 1 + k, c]), split(late_c[:, c * CHUNK : (c + 1) * CHUNK]), NT)
                value = term if value is None else value + term
            grad[corner, lanes - 2 + k] = -value
        pair_start(corner)

    def late_finish():
        def act(p, shift, g):
            chip_all(p, g).wait_recv()
            for b in range(lanes)[group(g)]:
                late_out[:, (b + shift) * lane : (b + shift + 1) * lane] = total(p, b)

        late_out[:, :lane] = jnp.zeros((part, lane), F32)
        groups(late, functools.partial(act, late, 0))
        groups(corner, functools.partial(act, corner, 2))
        late_result().start()

    def solve(p, c, own):
        y[p, c] = product((dth[p], dtl[p]), split(own), NN)

    def inverse(p):
        hi, lo = split(diag_ref[p].T)
        dth[p] = hi
        dtl[p] = lo

    def receive(p, c):
        root = n_row - 1 - p
        source = row == root
        if p == last:
            source = source | (row == helper)
        if p == last - 1:
            source = source | ((row == last_root) & ((c == RAW[0]) | (c == RAW[1])))
        if p == 1:
            source = source | (row == n_row - 1)
        for h in range(PIECES[p]):
            @pl.when(jnp.logical_not(source))
            def _():
                y_copy(p, c, h, down_sem, n_row - 1).wait_recv()

            @pl.when(jnp.logical_not(source) & (row > root) & (row < n_row - 1))
            def _():
                up(p, c, h).start()

            @pl.when((row > 0) & (row < root))
            def _():
                down(p, c, h).start()

    def send(p, c, way):
        for h in range(PIECES[p]):
            way(p, c, h).start()

    def tail_update(p, c):
        res_ref[tail:, columns(c)] -= product((pth[p, tail:], ptl[p, tail:]), split(y[p, c]), NN)

    def keep(p, c):
        @pl.when(row == n_row - 1 - p)
        def _():
            res_ref[tail:, columns(c)] = y[p, c]

    def grad_block(q, c, yq, b):
        at = slice(b * width, (b + 1) * width)
        value = product(yq, (wh[c, at], wl[c, at]), NT)
        grad[q, 2 * b] -= value[:, :lane]
        grad[q, 2 * b + 1] -= value[:, lane:]

    def grad_work(q, c):
        yq = split(y[q, c])
        for b in range(blocks):
            grad_block(q, c, yq, b)

    def grad_last(q, c):
        yq = split(y[q, c])
        for b in range(blocks):
            grad_block(q, c, yq, b)
            if q == last and b == blocks - 1:
                lower(q)
            for g in range(1, 4):
                if group(g).stop == 2 * b + 2:
                    pair_group(q, g)

    def res_work(q, c):
        yq = split(y[q, c])
        for b in range(blocks - 1):
            at = slice(b * width, (b + 1) * width)
            res_ref[at, columns(c)] -= product((pth[q, at], ptl[q, at]), yq, NN)

    def take_panels(n):
        panel_shares(n).wait_recv()
        for p in range(n):
            hi, lo = split(far_pan[p].T)
            fph[p] = hi
            fpl[p] = lo

    def far(q, c):
        far_rows(c, 1).wait_recv()
        own = far_own[c]
        for p in range(q):
            own = own - product((fph[p], fpl[p]), split(y[p, c]), NN)
        solve(q, c, own)

    def advance(p, c):
        root = n_row - 1 - p
        receive(p, c)

        @pl.when(row < root)
        def _():
            tail_update(p, c)

            @pl.when(row == root - 1)
            def _():
                solve(p + 1, c, res_ref[tail:, columns(c)])
                if p + 1 < last - 1:
                    send(p + 1, c, down)

                if p > 0:
                    send(p + 1, c, up)

        keep(p, c)

    def close(c):
        receive(last - 1, c)
        tail_update(last - 1, c)
        solve(last, c, res_ref[tail:, columns(c)])

        @pl.when(row > 0)
        def _():
            send(last, c, down)

        keep(last, c)
        for q in (last, last - 1):
            grad_work(q, c)
            res_work(q, c)

    barrier = pltpu.get_barrier_semaphore()
    for step in (1, n_row - 1):
        pl.semaphore_signal(barrier, inc=1, device_id={"row": lax.rem(row + step, n_row)}, device_id_type=MESH)
    for step in range(1, n_col):
        pl.semaphore_signal(barrier, inc=1, device_id={"col": lax.rem(col + step, n_col)}, device_id_type=MESH)

    diag_copy = pltpu.make_async_copy(diag_hbm, diag_ref, local_sem.at[0])
    tail_copy = pltpu.make_async_copy(cot_hbm.at[tail:], res_ref.at[tail:], local_sem.at[1])
    pan_copy = pltpu.make_async_copy(pan_hbm, pan_ref, local_sem.at[2])
    head_copy = pltpu.make_async_copy(cot_hbm.at[:tail], res_ref.at[:tail], local_sem.at[3])
    wht_copy = pltpu.make_async_copy(wht_hbm, wht_ref, local_sem.at[4])
    for copy in (diag_copy, tail_copy, pan_copy, wht_copy, head_copy):
        copy.start()
    pl.semaphore_wait(barrier, 2 + n_col - 1)

    @pl.when(row == helper)
    def _():
        panel_part(last - 1, n_row - 1).start()
        for c in RAW:
            far_rows(c, n_row - 1).start()

    @pl.when(row == n_row - 2)
    def _():
        panel_part(1, 1).start()

        @pl.loop(0, count)
        def _(c):
            far_rows(c, 1).start()

    @pl.when(row == last_root)
    def _():
        panel_part(last, 1).start()
        for c in range(LATE + 1):
            far_rows(c, 1).start()
        late_rows().start()

        @pl.loop(LATE + 1, count)
        def _(c):
            far_rows(c, 1).start()

        corner_rows().start()

    diag_copy.wait()
    inverse(0)
    tail_copy.wait()

    @pl.when(row == n_row - 1)
    def _():
        @pl.loop(0, count)
        def _(c):
            solve(0, c, res_ref[tail:, columns(c)])
            send(0, c, down)

    @pl.loop(1, panels)
    def _(p):
        inverse(p)

    pan_copy.wait()

    @pl.loop(0, panels)
    def _(p):
        for b in range(blocks):
            hi, lo = split(pan_ref[p, :, b * width : (b + 1) * width].T)
            pth[p, b * width : (b + 1) * width] = hi
            ptl[p, b * width : (b + 1) * width] = lo
        grad[p] = jnp.zeros(grad.shape[1:], F32)

    def share_panels(n, step):
        panel_part(n, step).wait_recv()
        for k in range(1, n_col):
            panel_share(n, k).start()

    @pl.when(row == helper)
    def _():
        share_panels(last, 1)

    @pl.when(row == last_root)
    def _():
        share_panels(last - 1, n_row - 1)

    @pl.when(row == n_row - 1)
    def _():
        share_panels(1, 1)

    wht_copy.wait()
    head_copy.wait()
    advance(0, 0)

    @pl.when(row == n_row - 1)
    def _():
        take_panels(1)

    @pl.when(row == helper)
    def _():
        take_panels(last)

    passing = (row > helper) & (row < n_row - 1)

    @pl.loop(0, count)
    def _(c):
        @pl.when(passing & (c == count - 1))
        def _():
            receive(last - 1, 0)

        hi, lo = split(wht_ref[:, columns(c)])
        wh[c] = hi
        wl[c] = lo
        grad_work(0, c)

        @pl.when(c == count - 1)
        def _():
            pair_start(0)

        res_work(0, c)

        @pl.when(c == count - 1)
        def _():
            chip_start(0)

        @pl.when(row == n_row - 1)
        def _():
            far(1, c)

        for p in range(1, last - 1):
            advance(p, c)

        @pl.when(row == helper)
        def _():
            @pl.when(c == count - 1)
            def _():
                @pl.loop(RAW[1] + 1, count)
                def _(k):
                    send(last - 1, k, down)

                send(last - 1, LATE, down)

            far(last, c)
            send(last, c, up)

            @pl.when(c == LATE + 1)
            def _():
                late_work()

        for q in range(1, last - 1):
            grad_work(q, c)

            @pl.when(c == count - 1)
            def _():
                pair_start(q)

            res_work(q, c)

        @pl.when(spared & (c >= 1) & (c <= 2))
        def _():
            @pl.when(c == 1)
            def _():
                take_panels(last - 1)

            r = (c - 1) * (RAW[1] - RAW[0]) + RAW[0]
            far(last - 1, r)
            close(r)

        @pl.when(c + 1 < count)
        def _():
            advance(0, c + 1)

        @pl.when(row == helper)
        def _():
            grad_work(last - 1, c)
            res_work(last - 1, c)

            @pl.when(c == LATE + 1)
            def _():
                chip_start(late)

    @pl.when(jnp.logical_not(passing))
    def _():
        for p in range(1, last - 1):
            chip_start(p)

    @pl.when(row == helper)
    def _():
        pair_start(last - 1)

    below = row < helper
    start = jnp.where(spared, len(RAW), 0)
    bulk = jnp.where(spared, count - 2, count - 1)

    @pl.loop(start, count)
    def _(t):
        c = jnp.where(below & (t > 0), jnp.where(t == count - 1, LATE, t + 1), t)

        @pl.when((row != helper) & ((t > 0) | jnp.logical_not(passing)))
        def _():
            receive(last - 1, c)

        @pl.when((row != helper) & jnp.logical_not(spared))
        def _():
            grad_work(last - 1, c)

            @pl.when(t == count - 1)
            def _():
                pair_start(last - 1)

        @pl.when(t > bulk)
        def _():
            grad_last(last - 1, c)

        @pl.when(below)
        def _():
            tail_update(last - 1, c)

            @pl.when(spared)
            def _():
                solve(last, c, res_ref[tail:, columns(c)])

                @pl.when(row > 0)
                def _():
                    send(last, c, down)

        @pl.when(t > bulk)
        def _():
            chip_start(last - 1)

        keep(last - 1, c)

        @pl.when(row > helper)
        def _():
            res_work(last - 1, c)

            @pl.when((row == n_row - 1) & (t == count - 1))
            def _():
                chip_start(last - 1)

        receive(last, c)

        @pl.when(passing & (t == 0))
        def _():
            for p in range(1, last - 1):
                chip_start(p)

        @pl.when(row < last_root)
        def _():
            tail_update(last, c)

        keep(last, c)

        @pl.when((row > helper) & (row < n_row - 1) & (t == count - 1) | (row == helper) & (t == 0))
        def _():
            chip_start(last - 1)

        @pl.when((t < bulk) | jnp.logical_not(spared))
        def _():
            grad_work(last, c)

            @pl.when(t == bulk)
            def _():
                pair_start(last)

        @pl.when(spared & (t == bulk))
        def _():
            grad_last(last, c)
            chip_start(last)

        @pl.when(spared & (t <= bulk))
        def _():
            grad_work(last - 1, c)

        @pl.when(row == helper)
        def _():
            @pl.when(t == 1)
            def _():
                corner_work()

            @pl.when(t == 2)
            def _():
                chip_start(corner)

        @pl.when(below)
        def _():
            res_work(last - 1, c)

        res_work(last, c)

    @pl.when(row < last_root)
    def _():
        chip_start(last - 1)

    @pl.when(jnp.logical_not(spared))
    def _():
        chip_start(last)

    for p in range(last - 1):
        finish(p)

    @pl.when(row == helper)
    def _():
        late_finish()

    @pl.loop(0, panels)
    def _(p):
        root = n_row - 1 - p
        groups(p, lambda g: pair_all(p, g).wait_send())

        @pl.when((row >= root) & (row < n_row - 1) & ((p < last) | (row > last_root)) & (p != 1))
        def _():
            y_all(p, 0, up_sem, 1).wait_send()

        @pl.when((row <= root) & (row > 0) & ((p != last - 1) | (row != helper)))
        def _():
            y_all(p, 0, down_sem, n_row - 1).wait_send()

    @pl.when(row == helper)
    def _():
        y_all(last - 1, len(RAW), down_sem, n_row - 1).wait_send()
        panel_part(last - 1, n_row - 1).wait_send()
        for c in RAW:
            far_rows(c, n_row - 1).wait_send()
        panel_shares(last).wait_send()
        for p in (late, corner):
            groups(p, lambda g: pair_all(p, g).wait_send())
            groups(p, lambda g: chip_all(p, g).wait_send())

    @pl.when(row == n_row - 2)
    def _():
        panel_part(1, 1).wait_send()
        own_all().wait_send()

    @pl.when(row == n_row - 1)
    def _():
        panel_shares(1).wait_send()

    @pl.when(spared)
    def _():
        panel_part(last, 1).wait_send()
        own_all().wait_send()
        panel_shares(last - 1).wait_send()
        late_rows().wait_send()
        corner_rows().wait_send()

    for p in range(last - 1):
        groups(p, lambda g: chip_all(p, g).wait_send())

    finish(last)

    @pl.when(spared)
    def _():
        late_result().wait_recv()
        out_ref[last - 1, :, :lane] = late_in[:, rows : rows + lane]
        out_ref[last, :, lane:] += late_in[:, lane:rows]
        out_ref[last, :, :lane] = late_in[:, rows + lane :]

    finish(last - 1)

    for p in (last - 1, last):
        groups(p, lambda g: chip_all(p, g).wait_send())

    @pl.when(row == helper)
    def _():
        late_result().wait_send()


def store_kernel(res_ref, grad_ref, res_hbm, grad_hbm, sems):
    step = res_ref.shape[0] // STORES
    copies = [pltpu.make_async_copy(grad_ref, grad_hbm, sems.at[STORES])]
    for k in range(STORES):
        at = slice(k * step, (k + 1) * step)
        copies.append(pltpu.make_async_copy(res_ref.at[at], res_hbm.at[at], sems.at[k]))
    for copy in copies:
        copy.start()
    for copy in copies:
        copy.wait()


def solution(mesh):
    n_row, n_col = mesh.shape["row"], mesh.shape["col"]

    def body(cotangent, whitened, panel_rows, diag_inverse):
        rows, rhs = cotangent.shape
        panels, width = diag_inverse.shape[:2]
        assert panels == len(PIECES) <= n_row and n_col % 2 == 0 and rhs // CHUNK > RAW[1] + 1
        count, blocks, part, chips = rhs // CHUNK, rows // width, width // n_col, n_col // 2
        anywhere = pl.BlockSpec(memory_space=pl.ANY)
        vmem = pl.BlockSpec(memory_space=pltpu.VMEM)
        hbm = pl.BlockSpec(memory_space=pltpu.HBM)
        dma = pltpu.SemaphoreType.DMA
        kept = pl.pallas_call(
            functools.partial(kernel, n_row, n_col),
            out_shape=(pltpu.VMEM((rows, rhs), F32), pltpu.VMEM((panels, part, rows), F32)),
            in_specs=[hbm] * 4,
            out_specs=(vmem, vmem),
            scratch_shapes=[
                pltpu.VMEM((rows, rhs), F32),
                pltpu.VMEM((panels, width, rows), F32),
                pltpu.VMEM((panels, width, width), F32),
                pltpu.VMEM((panels, count, width, CHUNK), F32),
                pltpu.VMEM((panels, rows, width), BF16),
                pltpu.VMEM((panels, rows, width), BF16),
                pltpu.VMEM((panels, width, width), BF16),
                pltpu.VMEM((panels, width, width), BF16),
                pltpu.VMEM((count, rows, CHUNK), BF16),
                pltpu.VMEM((count, rows, CHUNK), BF16),
                pltpu.VMEM((panels + 2, 2 * blocks, width, width // 2), F32),
                pltpu.VMEM((panels + 2, chips, 2 * blocks, part, width // 2), F32),
                pltpu.VMEM((panels + 2, chips, 2 * blocks, part, width // 2), F32),
                pltpu.VMEM((panels - 1, width, width), F32),
                pltpu.VMEM((count, width, CHUNK), F32),
                pltpu.VMEM((panels - 1, width, width), BF16),
                pltpu.VMEM((panels - 1, width, width), BF16),
                pltpu.VMEM((rows, CHUNK), F32),
                pltpu.VMEM((width // 2, rhs), F32),
                pltpu.VMEM((part, rows + width), F32),
                pltpu.VMEM((part, rows + width), F32),
                dma((5,)),
                dma((count, sum(PIECES))),
                dma,
                dma,
                dma,
                dma((3 * panels + 4,)),
                dma,
                dma((3 * panels + 4,)),
                dma,
                dma,
                dma((count,)),
                dma,
                dma,
                dma,
                dma,
            ],
            compiler_params=pltpu.CompilerParams(
                collective_id=0, has_side_effects=True, vmem_limit_bytes=117 * 512 * 1024
            ),
        )(cotangent, whitened, panel_rows, diag_inverse)
        return pl.pallas_call(
            store_kernel,
            out_shape=tuple(jax.ShapeDtypeStruct(k.shape, F32) for k in kept),
            in_specs=[anywhere] * 2,
            out_specs=(hbm, hbm),
            scratch_shapes=[dma((STORES + 1,))],
            compiler_params=pltpu.CompilerParams(vmem_limit_bytes=1024 * 1024),
        )(*kept)

    return jax.shard_map(
        body,
        mesh=mesh,
        in_specs=(P("row", "col"), P("row", "col"), P(None, None, "row"), P()),
        out_specs=(P("row", "col"), P(None, "col", "row")),
        check_vma=False,
    )
```
